256 devices in a mesh: dop: 64 (over y, z, core), rng: 4 (over x).
Axes of the slice: x: 4, y: 4, z: 8, core: 2. Of those that a mesh axis runs over, the one named last changes fastest.
Arguments:
- raw_echo: float32 [2, 512, 512, 128], P(None, 'dop', 'rng'), may hold values from -6 to 6
- replica: float32 [2, 64], replicated, may hold values from -0.5 to 0.5
- beam_weights: bfloat16 [2, 512, 192], replicated, may hold values from -0.1875 to 0.1875
- pivots: int32 [128, 192], replicated, may hold values from 0 to 191, each once within a row
- owner_counts: int32 [64], replicated, may hold values from 1 to 4, 128 in all
- train_gates: int32 [128, 256], P(None, 'rng'), may hold values from 0 to 511, as said below
Outputs:
- factor: float32 [256, 384, 384], P('dop', 'rng')
The draws below stay inside these ranges and needn't reach their ends.
Inputs may be any that keep to these rules, and one draw needn't show every extreme that they name: Owner o holds the run of owner_counts[o] consecutive Doppler bins that follows the bins of the owners below it; the counts sum to 128, and the largest is exactly 4 in every draw. `pivots`: each row is a permutation of 0 to 191. `train_gates`: in each row, columns r * 64 to (r + 1) * 64 - 1 hold distinct gates of range block r, that is of r * 128 to (r + 1) * 128 - 1.
All inputs are finite; a program needn't handle non-finite values.
Results may differ from the reference program's by a relative error of at most 0.005.
Values may be sent and summed in bfloat16 or wider, within the bound.
A program may use at most 64 MiB of HBM per device.

```python
import math
import jax
import jax.numpy as jnp
import numpy as np
from jax import lax

CH = 512
PULSES = 128
DOF = 192
TAPS = 64
GATES_DEV = 128
GATES = 512
TRAIN_DEV = 64
MOST = 4
N_DOP = 64


def draw_train_gates(key, part):
    block_count = GATES // GATES_DEV
    key_list = jax.random.split(key, PULSES * block_count)

    def choose_gates(one_key):
        return jax.random.permutation(one_key, GATES_DEV)[:TRAIN_DEV].astype(jnp.int32)
    local_gates = jax.vmap(choose_gates)(key_list).reshape(PULSES, block_count, TRAIN_DEV)
    block_start = (jnp.arange(block_count, dtype=jnp.int32) * GATES_DEV)[None, :, None]
    return (local_gates + block_start).reshape(PULSES, block_count * TRAIN_DEV)


def block_scale(rng, extent, cuts, low, top_value):
    loudness = 1.0
    for position, parts in cuts:
        draws = jax.random.uniform(jax.random.fold_in(jax.random.fold_in(rng, 6), position), (parts,), jnp.float32, low / len(cuts), top_value / len(cuts))
        loudness = loudness * jnp.repeat(jnp.exp(draws), extent[position] // parts).reshape((-1,) + (1,) * (len(extent) - 1 - position))
    return loudness


def length_profile(count, total, most, slope):
    weights = [(1 << 20) // math.isqrt(standing ** slope) + 1 for standing in range(2, count + 1)]
    rest, given = total - most - (count - 1), [1] * (count - 1)
    while rest > 0:
        movable = [i for i in range(count - 1) if given[i] < most]
        mass, budget = sum([weights[i] for i in movable]), rest
        for i in movable:
            addition = min(most - given[i], max(1, budget * weights[i] // mass), rest)
            given[i] = given[i] + addition
            rest = rest - addition
    return np.array([most] + given)


def ragged_sizes(own_key, number_of, total, reach, skew):
    if number_of == 2:
        one = jax.random.randint(own_key, (), max(1, total - reach), min(reach, total - 1) + 1)
        return jnp.stack([one, total - one])
    lengths = jnp.asarray(length_profile(number_of, total, reach, skew), jnp.int32)
    twos = (number_of - 1) // 2
    donor, sink = lengths[1:1 + 2 * twos:2], lengths[2:2 + 2 * twos:2]
    margin = jnp.minimum(donor - 1, reach - sink)
    passed = jax.random.randint(jax.random.fold_in(own_key, 1), (twos,), 0, 1 << 20) % (margin + 1)
    lengths = lengths.at[1:1 + 2 * twos:2].set(donor - passed).at[2:2 + 2 * twos:2].set(sink + passed)
    return lengths[jax.random.permutation(jax.random.fold_in(own_key, 2), number_of)]


def noise(rng, dims, width, bound, cuts=(), kind=jnp.bfloat16):
    loudness = block_scale(rng, dims, cuts, -0.22, 0.18) if cuts else 1.0
    result = jax.random.normal(rng, dims, jnp.float32) * width * loudness
    return jnp.minimum(jnp.maximum(result, -bound), bound).astype(kind)


def setup_inputs(seed: int = 0) -> dict:
    splits = jax.random.split(jax.random.key(seed), 7)
    return {
        "raw_echo": noise(splits[0], (2, CH, GATES, PULSES), 1.0, 6.0, ((1, 64), (2, 4)), jnp.float32),
        "replica": noise(splits[1], (2, TAPS), (2 * TAPS) ** -0.5, 0.5, (), jnp.float32),
        "beam_weights": noise(splits[2], (2, CH, DOF), (2 * CH) ** -0.5, 0.1875),
        "pivots": jax.vmap(lambda own: jax.random.permutation(own, DOF))(jax.random.split(splits[3], PULSES)).reshape((PULSES, DOF)).astype(jnp.int32),
        "owner_counts": ragged_sizes(splits[4], N_DOP, PULSES, MOST, 2).astype(jnp.int32),
        "train_gates": draw_train_gates(jax.random.fold_in(splits[6], 71), 0),
    }


LOADING = 0.25

def complex_block(real_part, imag_part):
    upper_row = jnp.stack([real_part, imag_part])
    lower_row = jnp.stack([-imag_part, real_part])
    return jnp.stack([upper_row, lower_row])

def doppler_table(pulse_count):
    pulse_index = jnp.arange(pulse_count, dtype=jnp.int32)
    phase_index = pulse_index[:, None] * pulse_index[None, :] % pulse_count
    angle_table = phase_index.astype(jnp.float32) * (2.0 * math.pi / pulse_count)
    norm_scale = 1.0 / math.sqrt(pulse_count)
    return complex_block(jnp.cos(angle_table) * norm_scale, jnp.sin(angle_table) * norm_scale)

def factor_matrix(real_part, imag_part, pivot_row, count_rows):
    real_part = real_part / count_rows
    imag_part = imag_part / count_rows
    real_pivot = jnp.take(jnp.take(real_part, pivot_row, axis=0), pivot_row, axis=1)
    imag_pivot = jnp.take(jnp.take(imag_part, pivot_row, axis=0), pivot_row, axis=1)
    upper_half = jnp.concatenate([real_pivot, -imag_pivot], axis=1)
    lower_half = jnp.concatenate([imag_pivot, real_pivot], axis=1)
    matrix = jnp.concatenate([upper_half, lower_half], axis=0)
    matrix = matrix + LOADING * jnp.eye(matrix.shape[0], dtype=matrix.dtype)
    return jnp.linalg.cholesky(matrix).T

def match_channel(echo_block, replica):
    tap_count = replica.shape[1]
    gate_count = echo_block.shape[1]
    padded = jnp.pad(echo_block, ((0, 0), (0, tap_count - 1), (0, 0)))
    real_sum = jnp.zeros(echo_block.shape[1:], echo_block.dtype)
    imag_sum = jnp.zeros(echo_block.shape[1:], echo_block.dtype)
    for tap_index in range(tap_count):
        window = padded[:, tap_index:tap_index + gate_count, :]
        real_sum = real_sum + replica[0, tap_index] * window[0] + replica[1, tap_index] * window[1]
        imag_sum = imag_sum + replica[0, tap_index] * window[1] - replica[1, tap_index] * window[0]
    return jnp.stack([real_sum, imag_sum])

def reference(raw_echo, replica, beam_weights, pivots, owner_counts, train_gates):
    dft_table = doppler_table(PULSES)

    def one_channel(channel_index):
        echo_block = lax.dynamic_index_in_dim(raw_echo, channel_index, 1, keepdims=False)
        matched = match_channel(echo_block, replica)
        spectra = jnp.einsum('abpk,bgp->kag', dft_table, matched, precision=lax.Precision.HIGHEST)
        return spectra.astype(jnp.bfloat16)
    spectrum = lax.map(one_channel, jnp.arange(CH, dtype=jnp.int32))
    weights = complex_block(beam_weights[0], beam_weights[1]).astype(jnp.float32)
    count_rows = float(train_gates.shape[1])

    def one_bin(bin_index):
        incoming = lax.dynamic_index_in_dim(spectrum, bin_index, 1, keepdims=False)
        gate_list = lax.dynamic_index_in_dim(train_gates, bin_index, 0, keepdims=False)
        chosen = jnp.take(incoming, gate_list, axis=2).astype(jnp.float32)
        beam_data = jnp.einsum('abcd,cbk->adk', weights, chosen).astype(jnp.bfloat16)
        stacked = beam_data.reshape(2 * DOF, -1)
        product = jnp.dot(stacked.astype(jnp.float32), stacked.T.astype(jnp.float32), preferred_element_type=jnp.float32)
        real_part = product[:DOF, :DOF] + product[DOF:, DOF:]
        imag_part = product[DOF:, :DOF] - product[:DOF, DOF:]
        pivot_row = lax.dynamic_index_in_dim(pivots, bin_index, 0, keepdims=False)
        return factor_matrix(real_part, imag_part, pivot_row, count_rows)
    factors = lax.map(one_bin, jnp.arange(PULSES, dtype=jnp.int32))
    starts = jnp.cumsum(owner_counts, dtype=jnp.int32) - owner_counts
    slot_index = jnp.arange(MOST, dtype=jnp.int32)
    slot_bins = jnp.minimum(starts[:, None] + slot_index[None, :], PULSES - 1).reshape(-1)
    filled = (slot_index[None, :] < owner_counts[:, None]).reshape(-1)
    placed = jnp.take(factors, slot_bins, axis=0)
    return jnp.where(filled[:, None, None], placed, 0.0)
```

```python
import functools
import math

import jax
import jax.numpy as jnp
import numpy as np
from jax import lax
from jax.experimental import pallas as pl
from jax.experimental.pallas import tpu as pltpu
from jax.sharding import PartitionSpec as P

LOADING = 0.25
MESH = pl.DeviceIdType.MESH
BF16 = jnp.bfloat16
F32 = jnp.float32


def doppler_table(pulse_count):
    index = np.arange(pulse_count, dtype=np.int32)
    phase = (index[:, None] * index[None, :]) % pulse_count
    angle = phase.astype(np.float32) * np.float32(2.0 * math.pi / pulse_count)
    scale = np.float32(1.0 / math.sqrt(pulse_count))
    cos, sin = np.cos(angle) * scale, np.sin(angle) * scale
    table = np.block([[cos, -sin], [sin, cos]]).astype(np.float32)
    high = table.astype(BF16)
    low = (table - high.astype(np.float32)).astype(BF16)
    return high, low


def halves(x):
    high = x.astype(BF16)
    return high, (x - high.astype(F32)).astype(BF16)


def dot(a, b, dims=((1,), (0,))):
    return lax.dot_general(a, b, (dims, ((), ())), preferred_element_type=F32)


def front_kernel(most, counts_ref, raw_ref, rim_ref, replica_ref, high_ref, low_ref, gates_ref, out_ref, spec_ref, pick_ref):
    _, channels, gates, pulses = raw_ref.shape
    rim = rim_ref.shape[2]
    taps = replica_ref.shape[1]
    chosen = gates_ref.shape[1]
    owners = out_ref.shape[0]
    table_high, table_low = high_ref[...], low_ref[...]

    local = gates_ref[...] % gates
    pick_ref[...] = jnp.concatenate([local, local], axis=1)

    lane = lax.broadcasted_iota(jnp.int32, (gates, gates), 1)
    row = lax.broadcasted_iota(jnp.int32, (gates, gates), 0)
    back = (gates - lane[:8]) % gates
    rolled = []
    for part in range(2):
        line = jnp.concatenate([replica_ref[part : part + 1], jnp.zeros((1, gates - taps), F32)], axis=1)
        line = jnp.take_along_axis(jnp.broadcast_to(line, (8, gates)), back, axis=1)
        rolled.append(pltpu.roll(jnp.broadcast_to(line[:1], (gates, gates)), 0, 1, stride=1, stride_axis=0))
    near = (row >= lane) & (row - lane < taps)
    far = (row[:rim] + gates - lane[:rim]) < taps
    re_near, im_near = [jnp.where(near, part, 0.0) for part in rolled]
    re_far, im_far = [jnp.where(far, part[:rim], 0.0) for part in rolled]
    response = jnp.concatenate(
        [
            jnp.concatenate([re_near, -im_near], axis=1),
            jnp.concatenate([im_near, re_near], axis=1),
            jnp.concatenate([re_far, -im_far], axis=1),
            jnp.concatenate([im_far, re_far], axis=1),
        ],
        axis=0,
    )
    resp_high, resp_low = halves(response)

    for c in range(channels):
        high, low = halves(jnp.concatenate([raw_ref[0, c], raw_ref[1, c]], axis=1))
        inner = dot(high, table_high) + (dot(low, table_high) + dot(high, table_low))
        edge = jnp.concatenate([rim_ref[0, c], rim_ref[1, c]], axis=1)
        outer = dot(edge, table_high) + dot(edge, table_low)
        stacked = jnp.concatenate(
            [inner[:, :pulses], inner[:, pulses:], outer[:, :pulses], outer[:, pulses:]], axis=0
        )
        high, low = halves(stacked)
        tn = ((0,), (0,))
        done = dot(high, resp_high, tn) + (dot(low, resp_high, tn) + dot(high, resp_low, tn))
        spec_ref[:, c, :] = done[:, :gates]
        spec_ref[:, channels + c, :] = done[:, gates:]

    last_bin = pulses - 1
    first_half = lax.broadcasted_iota(jnp.int32, (channels, 2 * chosen), 1) < chosen

    def one_owner(owner, start):
        for slot in range(most):
            b = jnp.minimum(start + slot, last_bin)
            index = jnp.broadcast_to(pick_ref[pl.ds(b, 1), :], (channels, 2 * chosen))
            real = jnp.take_along_axis(spec_ref[b, :channels], index, axis=1)
            imag = jnp.take_along_axis(spec_ref[b, channels:], index, axis=1)
            out_ref[owner, slot] = jnp.where(first_half, real, imag).astype(BF16)
        return start + counts_ref[owner]

    lax.fori_loop(0, owners, one_owner, 0)


def front(raw, rim, replica, gates, counts, most):
    _, channels, gate_rows, pulses = raw.shape
    owners = counts.shape[0]
    high, low = doppler_table(pulses)
    vmem = pl.BlockSpec(memory_space=pltpu.VMEM)
    return pl.pallas_call(
        functools.partial(front_kernel, most),
        out_shape=jax.ShapeDtypeStruct((owners, most, channels, 2 * gates.shape[1]), BF16),
        in_specs=[pl.BlockSpec(memory_space=pltpu.SMEM)] + [vmem] * 6,
        out_specs=vmem,
        scratch_shapes=[
            pltpu.VMEM((pulses, 2 * channels, gate_rows), F32),
            pltpu.VMEM((pulses, 2 * gates.shape[1]), jnp.int32),
        ],
        name="front",
    )(counts, raw, rim, replica, jnp.asarray(high), jnp.asarray(low), gates)


def factor_panel(a_ref, r_ref, t, full, k):
    base, off = 128 * t, 8 * k
    order = a_ref.shape[1]
    tiles = order // 128 - t
    sub = lax.broadcasted_iota(jnp.int32, (8, 128), 0)
    lane = lax.broadcasted_iota(jnp.int32, (8, 128), 1)
    r0 = pl.multiple_of(base + off, 8)
    p = [a_ref[pl.ds(r0, 8), base + 128 * u : base + 128 * u + 128] for u in range(tiles)]
    cols = [jnp.take_along_axis(p[0], jnp.full((8, 128), off + j, jnp.int32), axis=1) for j in range(8)]
    s = {(i, j): jnp.broadcast_to(cols[j][i : i + 1], (8, 128)) for j in range(8) for i in range(j + 1)}
    rows = [[jnp.broadcast_to(p[u][j : j + 1], (8, 128)) for j in range(8)] for u in range(tiles)]
    for j in range(8):
        inv = lax.rsqrt(s[j, j])
        up = {m: s[j, m] * inv for m in range(j + 1, 8)}
        for i in range(j + 1, 8):
            for m in range(i, 8):
                s[i, m] = s[i, m] - up[i] * up[m]
        for u in range(tiles):
            rows[u][j] = rows[u][j] * inv
            for i in range(j + 1, 8):
                rows[u][i] = rows[u][i] - up[i] * rows[u][j]
    x = []
    for u in range(tiles):
        v = rows[u][0]
        for j in range(1, 8):
            v = jnp.where(sub == j, rows[u][j], v)
        if u == 0:
            v = jnp.where(lane >= off + sub, v, 0.0)
        x.append(v)
        r_ref[pl.ds(r0, 8), base + 128 * u : base + 128 * u + 128] = v * full
    x = jnp.concatenate(x, axis=1)
    high = x.astype(BF16).astype(F32)
    low = x - high
    pad = jnp.zeros_like(x)
    lhs = jnp.concatenate([high[:, :128], high[:, :128], low[:, :128], pad[:, :128]], axis=0).astype(BF16)
    rhs = jnp.concatenate([high, low, high, pad], axis=0).astype(BF16)
    a_ref[base : base + 128, base:] = a_ref[base : base + 128, base:] - dot(lhs, rhs, ((0,), (0,)))


def factor_trailing(a_ref, r_ref, t):
    base, end = 128 * t, 128 * t + 128
    high, low = halves(r_ref[base:end, end:])
    tn = ((0,), (0,))
    update = dot(high, high, tn) + (dot(low, high, tn) + dot(high, low, tn))
    a_ref[end:, end:] = a_ref[end:, end:] - update


def back_kernel(
    count_rows, sizes, counts_ref, src_ref, weights_ref, pivots_ref, out_ref,
    recv_ref, bsend_ref, brecv_ref, a_ref, r_ref,
    local_sem, send_sem, recv_sem, bsend_sem, brecv_sem, rsend_sem, rrecv_sem,
):
    ny, nz, nc, nx = sizes
    owners = ny * nz * nc
    dop, rng = lax.axis_index("dop"), lax.axis_index("rng")
    y, z, c = dop // (nz * nc), (dop // nc) % nz, dop % nc

    def peer(k):
        kc, kz, ky = k % nc, (k // nc) % nz, k // (nc * nz)
        return (((y + ky) % ny) * nz + (z + kz) % nz) * nc + (c + kc) % nc

    barrier = pltpu.get_barrier_semaphore()

    def greet(k, carry):
        pl.semaphore_signal(barrier, inc=1, device_id=(peer(k), rng), device_id_type=MESH)
        return carry

    lax.fori_loop(1, owners, greet, 0)
    for k in range(1, nx):
        pl.semaphore_signal(barrier, inc=1, device_id=(dop, (rng + k) % nx), device_id_type=MESH)
    pl.semaphore_wait(barrier, owners - 1 + nx - 1)

    def send(k, carry):
        other = peer(k)
        pltpu.make_async_remote_copy(
            src_ref=src_ref.at[other], dst_ref=recv_ref.at[dop], send_sem=send_sem, recv_sem=recv_sem,
            device_id=(other, rng), device_id_type=MESH,
        ).start()
        return carry

    lax.fori_loop(1, owners, send, 0)
    own = pltpu.make_async_copy(src_ref.at[dop], recv_ref.at[dop], local_sem)
    own.start()

    start = lax.fori_loop(0, owners, lambda o, total: total + jnp.where(o < dop, counts_ref[o], 0), 0)
    slot_bin = jnp.minimum(start + rng, pivots_ref.shape[0] - 1)
    full = jnp.where(rng < counts_ref[dop], 1.0, 0.0)
    dof = pivots_ref.shape[1]
    order = 2 * dof
    pivot = pivots_ref[pl.ds(slot_bin, 1), :]
    chooser = (lax.broadcasted_iota(jnp.int32, (dof, dof), 0) == jnp.broadcast_to(pivot, (dof, dof))).astype(BF16)
    r_ref[...] = jnp.zeros_like(r_ref)

    own.wait()
    others = recv_ref.at[pl.ds(0, owners - 1)]
    pltpu.make_async_copy(others, others, recv_sem).wait()
    pltpu.make_async_copy(others, others, send_sem).wait()

    w_real, w_imag = weights_ref[0], weights_ref[1]
    channels = w_real.shape[0]
    wide = recv_ref.shape[3]
    sign = jnp.where(lax.broadcasted_iota(jnp.int32, (dof, wide), 1) < wide // 2, 1.0, -1.0)
    tn = ((0,), (0,))
    for k in range(1, nx + 1):
        slot = (rng + k) % nx
        data = recv_ref[:, slot].reshape(channels, wide)
        beams = dot(w_real, data, tn) + sign * pltpu.roll(dot(w_imag, data, tn), wide // 2, 1)
        if k < nx:
            bsend_ref[k - 1] = beams.astype(BF16)
            pltpu.make_async_remote_copy(
                src_ref=bsend_ref.at[k - 1], dst_ref=brecv_ref.at[rng], send_sem=bsend_sem.at[k - 1],
                recv_sem=brecv_sem.at[k - 1], device_id=(dop, slot), device_id_type=MESH,
            ).start()
        else:
            brecv_ref[rng] = beams.astype(BF16)
    for k in range(1, nx):
        pltpu.make_async_copy(bsend_ref.at[k - 1], bsend_ref.at[k - 1], bsend_sem.at[k - 1]).wait()
        pltpu.make_async_copy(bsend_ref.at[k - 1], bsend_ref.at[k - 1], brecv_sem.at[k - 1]).wait()

    parts = []
    for k in range(nx):
        parts.append(dot(chooser, brecv_ref[k], tn))
    upper = jnp.concatenate(parts, axis=1)
    lower = jnp.concatenate([sign * pltpu.roll(part, wide // 2, 1) for part in parts], axis=1)
    both = jnp.concatenate([upper, lower], axis=0).astype(BF16)
    gram = dot(both, both, ((1,), (1,)))
    diagonal = lax.broadcasted_iota(jnp.int32, (order, order), 0) == lax.broadcasted_iota(jnp.int32, (order, order), 1)
    a_ref[...] = gram * (1.0 / count_rows) + jnp.where(diagonal, LOADING, 0.0)

    rows = order // nx

    def piece(r, ref):
        first = (rows * r) // 128 * 128
        return ref.at[:, first:] if first else ref

    def deliver(r):
        @pl.when(rng != r)
        def _():
            pltpu.make_async_remote_copy(
                src_ref=piece(r, r_ref.at[pl.ds(rows * r, rows)]), dst_ref=piece(r, out_ref.at[rng]),
                send_sem=rsend_sem.at[r], recv_sem=rrecv_sem.at[rng],
                device_id=(dop, r), device_id_type=MESH,
            ).start()

    for r in range(nx):
        first = (rows * r) // 128 * 128
        if first:
            @pl.when(rng == r)
            def _():
                out_ref[:, :, :first] = jnp.zeros((nx, rows, first), F32)

    sent = 0
    for t in range(order // 128):
        k = 0
        while k < 16:
            stop = 16
            if sent < nx and rows * (sent + 1) <= 128 * t + 128:
                stop = (rows * (sent + 1) - 128 * t) // 8
            lax.fori_loop(k, stop, lambda i, carry: (factor_panel(a_ref, r_ref, t, full, i), carry)[1], 0)
            if 128 * t + 8 * stop == rows * (sent + 1):
                deliver(sent)
                sent += 1
            k = stop
        if t + 1 < order // 128:
            factor_trailing(a_ref, r_ref, t)

    for r in range(nx):
        @pl.when(rng == r)
        def _():
            out_ref[r] = r_ref[rows * r : rows * r + rows]
            for s in range(nx):
                if s != r:
                    done = piece(r, out_ref.at[s])
                    pltpu.make_async_copy(done, done, rrecv_sem.at[s]).wait()

        @pl.when(rng != r)
        def _():
            left = piece(r, r_ref.at[pl.ds(rows * r, rows)])
            pltpu.make_async_copy(left, left, rsend_sem.at[r]).wait()


def back(outgoing, weights, pivots, counts, count_rows, sizes):
    owners, most, channels, wide = outgoing.shape
    nx = sizes[3]
    dof = pivots.shape[1]
    order = 2 * dof
    vmem = pl.BlockSpec(memory_space=pltpu.VMEM)
    dma = pltpu.SemaphoreType.DMA
    return pl.pallas_call(
        functools.partial(back_kernel, count_rows, sizes),
        out_shape=jax.ShapeDtypeStruct((most, order // nx, order), F32),
        in_specs=[pl.BlockSpec(memory_space=pltpu.SMEM)] + [vmem] * 3,
        out_specs=vmem,
        scratch_shapes=[
            pltpu.VMEM((owners, most, channels, wide), BF16),
            pltpu.VMEM((nx - 1, dof, wide), BF16),
            pltpu.VMEM((nx, dof, wide), BF16),
            pltpu.VMEM((order, order), F32),
            pltpu.VMEM((order, order), F32),
            dma, dma, dma, dma((nx - 1,)), dma((nx - 1,)), dma((nx,)), dma((nx,)),
        ],
        compiler_params=pltpu.CompilerParams(collective_id=1, has_side_effects=True),
        name="back",
    )(counts, outgoing, weights, pivots)


def shifted(array, axis, by):
    count = lax.axis_size(axis)
    pairs = [(i, i + by) for i in range(count) if 0 <= i + by < count]
    return lax.ppermute(array, axis, pairs)


def local(sizes, raw_echo, replica, beam_weights, pivots, owner_counts, train_gates):
    pulses = raw_echo.shape[3]
    taps = replica.shape[1]
    ranges = lax.axis_size("rng")
    most = 2 * (pulses // owner_counts.shape[0])
    rim = shifted(raw_echo[:, :, :taps, :].astype(BF16), "rng", -1)
    outgoing = front(raw_echo, rim, replica, train_gates, owner_counts, most)
    count_rows = float(train_gates.shape[1] * ranges)
    return back(outgoing, beam_weights, pivots, owner_counts, count_rows, sizes)


def solution(mesh):
    return jax.shard_map(
        functools.partial(local, (4, 8, 2, 4)),
        mesh=mesh,
        in_specs=(P(None, "dop", "rng", None), P(), P(), P(), P(), P(None, "rng")),
        out_specs=P("dop", "rng", None),
        check_vma=False,
    )
```

```python
import functools
import math

import jax
import jax.numpy as jnp
import numpy as np
from jax import lax
from jax.experimental import pallas as pl
from jax.experimental.pallas import tpu as pltpu
from jax.sharding import PartitionSpec as P

LOADING = 0.25
MESH = pl.DeviceIdType.MESH
BF16 = jnp.bfloat16
F32 = jnp.float32


def doppler_table(pulse_count):
    index = np.arange(pulse_count, dtype=np.int32)
    phase = (index[:, None] * index[None, :]) % pulse_count
    angle = phase.astype(np.float32) * np.float32(2.0 * math.pi / pulse_count)
    scale = np.float32(1.0 / math.sqrt(pulse_count))
    cos, sin = np.cos(angle) * scale, np.sin(angle) * scale
    table = np.block([[cos, -sin], [sin, cos]]).astype(np.float32)
    high = table.astype(BF16)
    low = (table - high.astype(np.float32)).astype(BF16)
    return high, low


def halves(x):
    high = x.astype(BF16)
    return high, (x - high.astype(F32)).astype(BF16)


def dot(a, b, dims=((1,), (0,))):
    return lax.dot_general(a, b, (dims, ((), ())), preferred_element_type=F32)


def factor_panel(a_ref, r_ref, t, full, k):
    base, off = 128 * t, 8 * k
    order = a_ref.shape[1]
    tiles = order // 128 - t
    sub = lax.broadcasted_iota(jnp.int32, (8, 128), 0)
    lane = lax.broadcasted_iota(jnp.int32, (8, 128), 1)
    r0 = pl.multiple_of(base + off, 8)
    p = [a_ref[pl.ds(r0, 8), base + 128 * u : base + 128 * u + 128] for u in range(tiles)]
    cols = [jnp.take_along_axis(p[0], jnp.full((8, 128), off + j, jnp.int32), axis=1) for j in range(8)]
    s = {(i, j): jnp.broadcast_to(cols[j][i : i + 1], (8, 128)) for j in range(8) for i in range(j + 1)}
    rows = [[jnp.broadcast_to(p[u][j : j + 1], (8, 128)) for j in range(8)] for u in range(tiles)]
    for j in range(8):
        inv = lax.rsqrt(s[j, j])
        up = {m: s[j, m] * inv for m in range(j + 1, 8)}
        for i in range(j + 1, 8):
            for m in range(i, 8):
                s[i, m] = s[i, m] - up[i] * up[m]
        for u in range(tiles):
            rows[u][j] = rows[u][j] * inv
            for i in range(j + 1, 8):
                rows[u][i] = rows[u][i] - up[i] * rows[u][j]
    x = []
    for u in range(tiles):
        v = rows[u][0]
        for j in range(1, 8):
            v = jnp.where(sub == j, rows[u][j], v)
        if u == 0:
            v = jnp.where(lane >= off + sub, v, 0.0)
        x.append(v)
        r_ref[pl.ds(r0, 8), base + 128 * u : base + 128 * u + 128] = v * full
    x = jnp.concatenate(x, axis=1)
    high = x.astype(BF16).astype(F32)
    low = x - high
    pad = jnp.zeros_like(x)
    lhs = jnp.concatenate([high[:, :128], high[:, :128], low[:, :128], pad[:, :128]], axis=0).astype(BF16)
    rhs = jnp.concatenate([high, low, high, pad], axis=0).astype(BF16)
    a_ref[base : base + 128, base:] = a_ref[base : base + 128, base:] - dot(lhs, rhs, ((0,), (0,)))


def factor_trailing(a_ref, r_ref, t):
    base, end = 128 * t, 128 * t + 128
    high, low = halves(r_ref[base:end, end:])
    tn = ((0,), (0,))
    update = dot(high, high, tn) + (dot(low, high, tn) + dot(high, low, tn))
    a_ref[end:, end:] = a_ref[end:, end:] - update


def filter_response(replica_ref, gates, rim):
    taps = replica_ref.shape[1]
    lane = lax.broadcasted_iota(jnp.int32, (gates, gates), 1)
    row = lax.broadcasted_iota(jnp.int32, (gates, gates), 0)
    back = (gates - lane[:8]) % gates
    rolled = []
    for part in range(2):
        line = jnp.concatenate([replica_ref[part : part + 1], jnp.zeros((1, gates - taps), F32)], axis=1)
        line = jnp.take_along_axis(jnp.broadcast_to(line, (8, gates)), back, axis=1)
        rolled.append(pltpu.roll(jnp.broadcast_to(line[:1], (gates, gates)), 0, 1, stride=1, stride_axis=0))
    near = (row >= lane) & (row - lane < taps)
    far = (row[:rim] + gates - lane[:rim]) < taps
    re_near, im_near = [jnp.where(near, part, 0.0) for part in rolled]
    re_far, im_far = [jnp.where(far, part[:rim], 0.0) for part in rolled]
    return (
        jnp.concatenate(
            [jnp.concatenate([re_near, -im_near], axis=1), jnp.concatenate([im_near, re_near], axis=1)], axis=0
        ),
        jnp.concatenate(
            [jnp.concatenate([re_far, -im_far], axis=1), jnp.concatenate([im_far, re_far], axis=1)], axis=0
        ),
    )


def kernel(
    count_rows, sizes, counts_ref, replica_ref, raw_hbm, high_hbm, low_hbm, weights_hbm, pivots_hbm, gates_hbm, out_ref,
    raw_ref, high_ref, low_ref, weights_ref, pivots_ref, gates_ref,
    rim_out_ref, rim_in_ref, part_ref, spec_ref, pick_ref, starts_ref,
    pack_ref, recv_ref, bsend_ref, brecv_ref, a_ref, r_ref,
    load_sem, rim_send_sem, rim_recv_sem, send_sem, recv_sem, bsend_sem, brecv_sem, rsend_sem, rrecv_sem,
):
    ny, nz, nc, nx = sizes
    owners = ny * nz * nc
    _, channels, gates, pulses = raw_ref.shape
    rim = rim_in_ref.shape[2]
    most, wide = pack_ref.shape[1], pack_ref.shape[3]
    dop, rng = lax.axis_index("dop"), lax.axis_index("rng")
    y, z, c = dop // (nz * nc), (dop // nc) % nz, dop % nc
    tn = ((0,), (0,))

    def owner_at(ky, kz, kc):
        return (((y + ky) % ny) * nz + (z + kz) % nz) * nc + (c + kc) % nc

    loads = [
        pltpu.make_async_copy(raw_hbm.at[:, :, :rim], raw_ref.at[:, :, :rim], load_sem.at[0]),
        pltpu.make_async_copy(high_hbm, high_ref, load_sem.at[1]),
        pltpu.make_async_copy(low_hbm, low_ref, load_sem.at[2]),
        pltpu.make_async_copy(raw_hbm.at[:, :, rim:], raw_ref.at[:, :, rim:], load_sem.at[3]),
        pltpu.make_async_copy(gates_hbm, gates_ref, load_sem.at[4]),
        pltpu.make_async_copy(pivots_hbm, pivots_ref, load_sem.at[5]),
        pltpu.make_async_copy(weights_hbm, weights_ref, load_sem.at[6]),
    ]
    for load in loads:
        load.start()

    barrier = pltpu.get_barrier_semaphore()
    for k in range(1, nx):
        pl.semaphore_signal(barrier, inc=1, device_id=(dop, (rng + k) % nx), device_id_type=MESH)

    def greet(k, carry):
        other = owner_at(k // (nc * nz), (k // nc) % nz, k % nc)
        pl.semaphore_signal(barrier, inc=1, device_id=(other, rng), device_id_type=MESH)
        return carry

    lax.fori_loop(1, owners, greet, 0)

    loads[0].wait()
    for ch in range(channels):
        for part in range(2):
            rim_out_ref[ch, part] = raw_ref[part, ch, :rim].astype(BF16)

    pl.semaphore_wait(barrier, owners - 1 + nx - 1)

    @pl.when(rng > 0)
    def _():
        for ch in range(channels):
            pltpu.make_async_remote_copy(
                src_ref=rim_out_ref.at[ch], dst_ref=rim_in_ref.at[ch], send_sem=rim_send_sem.at[ch],
                recv_sem=rim_recv_sem.at[ch], device_id=(dop, rng - 1), device_id_type=MESH,
            ).start()

    @pl.when(rng == nx - 1)
    def _():
        rim_in_ref[...] = jnp.zeros_like(rim_in_ref)

    near, far = filter_response(replica_ref, gates, rim)
    near_high, near_low = halves(near)
    far_high, far_low = halves(far)
    for load in loads[1:4]:
        load.wait()
    for ch in range(channels):
        high, low = halves(jnp.concatenate([raw_ref[0, ch], raw_ref[1, ch]], axis=1))
        inner = dot(high, high_ref[...]) + (dot(low, high_ref[...]) + dot(high, low_ref[...]))
        high, low = halves(jnp.concatenate([inner[:, :pulses], inner[:, pulses:]], axis=0))
        part_ref[ch] = dot(high, near_high, tn) + (dot(low, near_high, tn) + dot(high, near_low, tn))

    def run(owner, total):
        starts_ref[owner] = total
        return total + counts_ref[owner]

    lax.fori_loop(0, owners, run, 0)
    loads[4].wait()
    local = gates_ref[...].T % gates
    pick_ref[...] = jnp.concatenate([local, local], axis=1)

    for ch in range(channels):
        @pl.when(rng < nx - 1)
        def _():
            pltpu.make_async_copy(rim_in_ref.at[ch], rim_in_ref.at[ch], rim_recv_sem.at[ch]).wait()

        edge = jnp.concatenate([rim_in_ref[ch, 0], rim_in_ref[ch, 1]], axis=1)
        outer = dot(edge, high_ref[...]) + dot(edge, low_ref[...])
        high, low = halves(jnp.concatenate([outer[:, :pulses], outer[:, pulses:]], axis=0))
        done = dot(high, far_high, tn) + (dot(low, far_high, tn) + dot(high, far_low, tn))
        done = done + part_ref[ch]
        spec_ref[:, ch, :] = done[:, :gates]
        spec_ref[:, channels + ch, :] = done[:, gates:]

    first_half = lax.broadcasted_iota(jnp.int32, (channels, wide), 1) < wide // 2

    def pack(owner, ref):
        for slot in range(most):
            b = jnp.minimum(starts_ref[owner] + slot, pulses - 1)
            index = jnp.broadcast_to(pick_ref[pl.ds(b, 1), :], (channels, wide))
            real = jnp.take_along_axis(spec_ref[b, :channels], index, axis=1)
            imag = jnp.take_along_axis(spec_ref[b, channels:], index, axis=1)
            ref[owner, slot] = jnp.where(first_half, real, imag).astype(BF16)

    def send(owner):
        pltpu.make_async_remote_copy(
            src_ref=pack_ref.at[owner], dst_ref=recv_ref.at[dop], send_sem=send_sem, recv_sem=recv_sem,
            device_id=(owner, rng), device_id_type=MESH,
        ).start()

    steps = ny * nc
    for kz in sorted(range(nz), key=lambda k: (min(k, nz - k), k)):
        def at(i, kz=kz):
            return owner_at(i % ny, kz, i // ny)

        first = 0 if kz else 1
        pack(at(first), pack_ref)

        def one(i, carry):
            pack(at(i), pack_ref)
            send(at(i - 1))
            return carry

        lax.fori_loop(first + 1, steps, one, 0)
        send(at(steps - 1))
    pack(dop, recv_ref)

    loads[5].wait()
    loads[6].wait()
    dof = pivots_ref.shape[0]
    order = 2 * dof
    slot_bin = jnp.minimum(starts_ref[dop] + rng, pulses - 1)
    full = jnp.where(rng < counts_ref[dop], 1.0, 0.0)
    pivot = jnp.take_along_axis(pivots_ref[...], jnp.full(pivots_ref.shape, slot_bin, jnp.int32), axis=1)
    pivot = jnp.concatenate([pivot, pivot], axis=1)[:, :dof]
    chooser = (lax.broadcasted_iota(jnp.int32, (dof, dof), 1) == pivot).astype(BF16)
    r_ref[...] = jnp.zeros_like(r_ref)
    rows = order // nx
    for r in range(nx):
        first = (rows * r) // 128 * 128
        if first:
            @pl.when(rng == r)
            def _():
                out_ref[:, :, :first] = jnp.zeros((nx, rows, first), F32)

    others = recv_ref.at[pl.ds(0, owners - 1)]
    pltpu.make_async_copy(others, others, recv_sem).wait()

    sign = jnp.where(lax.broadcasted_iota(jnp.int32, (dof, wide), 1) < wide // 2, 1.0, -1.0)
    for k in range(1, nx + 1):
        slot = (rng + k) % nx
        data = recv_ref[:, slot].reshape(owners * channels, wide)
        beams = dot(weights_ref[0], data) + sign * pltpu.roll(dot(weights_ref[1], data), wide // 2, 1)
        if k < nx:
            bsend_ref[k - 1] = beams.astype(BF16)
            pltpu.make_async_remote_copy(
                src_ref=bsend_ref.at[k - 1], dst_ref=brecv_ref.at[rng], send_sem=bsend_sem.at[k - 1],
                recv_sem=brecv_sem.at[k - 1], device_id=(dop, slot), device_id_type=MESH,
            ).start()
        else:
            brecv_ref[rng] = beams.astype(BF16)
    for k in range(1, nx):
        pltpu.make_async_copy(bsend_ref.at[k - 1], bsend_ref.at[k - 1], brecv_sem.at[k - 1]).wait()

    parts = [dot(chooser, brecv_ref[k]) for k in range(nx)]
    upper = jnp.concatenate(parts, axis=1)
    lower = jnp.concatenate([sign * pltpu.roll(part, wide // 2, 1) for part in parts], axis=1)
    both = jnp.concatenate([upper, lower], axis=0).astype(BF16)
    gram = dot(both, both, ((1,), (1,)))
    diagonal = lax.broadcasted_iota(jnp.int32, (order, order), 0) == lax.broadcasted_iota(jnp.int32, (order, order), 1)
    a_ref[...] = gram * (1.0 / count_rows) + jnp.where(diagonal, LOADING, 0.0)

    def piece(r, ref):
        first = (rows * r) // 128 * 128
        return ref.at[:, first:] if first else ref

    def deliver(r):
        @pl.when(rng != r)
        def _():
            pltpu.make_async_remote_copy(
                src_ref=piece(r, r_ref.at[pl.ds(rows * r, rows)]), dst_ref=piece(r, out_ref.at[rng]),
                send_sem=rsend_sem.at[r], recv_sem=rrecv_sem.at[rng],
                device_id=(dop, r), device_id_type=MESH,
            ).start()

    sent = 0
    for t in range(order // 128):
        k = 0
        while k < 16:
            stop = 16
            if sent < nx and rows * (sent + 1) <= 128 * t + 128:
                stop = (rows * (sent + 1) - 128 * t) // 8
            lax.fori_loop(k, stop, lambda i, carry: (factor_panel(a_ref, r_ref, t, full, i), carry)[1], 0)
            if 128 * t + 8 * stop == rows * (sent + 1):
                deliver(sent)
                sent += 1
            k = stop
        if t + 1 < order // 128:
            factor_trailing(a_ref, r_ref, t)

    pltpu.make_async_copy(others, others, send_sem).wait()
    for k in range(1, nx):
        pltpu.make_async_copy(bsend_ref.at[k - 1], bsend_ref.at[k - 1], bsend_sem.at[k - 1]).wait()

    @pl.when(rng > 0)
    def _():
        for ch in range(channels):
            pltpu.make_async_copy(rim_out_ref.at[ch], rim_out_ref.at[ch], rim_send_sem.at[ch]).wait()

    for r in range(nx):
        @pl.when(rng == r)
        def _():
            out_ref[r] = r_ref[rows * r : rows * r + rows]
            for s in range(nx):
                if s != r:
                    done = piece(r, out_ref.at[s])
                    pltpu.make_async_copy(done, done, rrecv_sem.at[s]).wait()

        @pl.when(rng != r)
        def _():
            left = piece(r, r_ref.at[pl.ds(rows * r, rows)])
            pltpu.make_async_copy(left, left, rsend_sem.at[r]).wait()


def local(sizes, raw_echo, replica, beam_weights, pivots, owner_counts, train_gates):
    _, channels, gates, pulses = raw_echo.shape
    taps = replica.shape[1]
    owners = owner_counts.shape[0]
    nx = sizes[3]
    dof = pivots.shape[1]
    order = 2 * dof
    chosen = train_gates.shape[1]
    most = 2 * (pulses // owners)
    count_rows = float(chosen * nx)
    high, low = doppler_table(pulses)
    weights, pivots, picks = beam_weights.transpose(0, 2, 1), pivots.T, train_gates.T
    vmem, anywhere = pl.BlockSpec(memory_space=pltpu.VMEM), pl.BlockSpec(memory_space=pl.ANY)
    dma = pltpu.SemaphoreType.DMA
    return pl.pallas_call(
        functools.partial(kernel, count_rows, sizes),
        out_shape=jax.ShapeDtypeStruct((most, order // nx, order), F32),
        in_specs=[pl.BlockSpec(memory_space=pltpu.SMEM), vmem] + [anywhere] * 6,
        out_specs=vmem,
        scratch_shapes=[
            pltpu.VMEM(raw_echo.shape, F32),
            pltpu.VMEM(high.shape, BF16),
            pltpu.VMEM(low.shape, BF16),
            pltpu.VMEM(weights.shape, BF16),
            pltpu.VMEM(pivots.shape, jnp.int32),
            pltpu.VMEM(picks.shape, jnp.int32),
            pltpu.VMEM((channels, 2, taps, pulses), BF16),
            pltpu.VMEM((channels, 2, taps, pulses), BF16),
            pltpu.VMEM((channels, pulses, 2 * gates), F32),
            pltpu.VMEM((pulses, 2 * channels, gates), F32),
            pltpu.VMEM((pulses, 2 * chosen), jnp.int32),
            pltpu.SMEM((owners,), jnp.int32),
            pltpu.VMEM((owners, most, channels, 2 * chosen), BF16),
            pltpu.VMEM((owners, most, channels, 2 * chosen), BF16),
            pltpu.VMEM((nx - 1, dof, 2 * chosen), BF16),
            pltpu.VMEM((nx, dof, 2 * chosen), BF16),
            pltpu.VMEM((order, order), F32),
            pltpu.VMEM((order, order), F32),
            dma((7,)), dma((channels,)), dma((channels,)), dma, dma,
            dma((nx - 1,)), dma((nx - 1,)), dma((nx,)), dma((nx,)),
        ],
        compiler_params=pltpu.CompilerParams(collective_id=1, has_side_effects=True),
        name="factors",
    )(owner_counts, replica, raw_echo, jnp.asarray(high), jnp.asarray(low), weights, pivots, picks)


def solution(mesh):
    return jax.shard_map(
        functools.partial(local, (4, 8, 2, 4)),
        mesh=mesh,
        in_specs=(P(None, "dop", "rng", None), P(), P(), P(), P(), P(None, "rng")),
        out_specs=P("dop", "rng", None),
        check_vma=False,
    )
```

```python
import functools
import math

import jax
import jax.numpy as jnp
import numpy as np
from jax import lax
from jax.experimental import pallas as pl
from jax.experimental.pallas import tpu as pltpu
from jax.sharding import PartitionSpec as P

LOADING = 0.25
MESH = pl.DeviceIdType.MESH
BF16 = jnp.bfloat16
F32 = jnp.float32


def doppler_table(pulse_count):
    index = np.arange(pulse_count, dtype=np.int32)
    phase = (index[:, None] * index[None, :]) % pulse_count
    angle = phase.astype(np.float32) * np.float32(2.0 * math.pi / pulse_count)
    scale = np.float32(1.0 / math.sqrt(pulse_count))
    cos, sin = np.cos(angle) * scale, np.sin(angle) * scale
    table = np.block([[cos, -sin], [sin, cos]]).astype(np.float32)
    high = table.astype(BF16)
    low = (table - high.astype(np.float32)).astype(BF16)
    return high, low


def halves(x):
    high = x.astype(BF16)
    return high, (x - high.astype(F32)).astype(BF16)


def dot(a, b, dims=((1,), (0,))):
    return lax.dot_general(a, b, (dims, ((), ())), preferred_element_type=F32)


def factor_rows(a_ref, r_ref, r0, full, span):
    order = a_ref.shape[1]
    edge = r0 // 128 * 128
    tiles, groups = (order - edge) // 128, span // 8
    shape = (8, 128)
    sub = lax.broadcasted_iota(jnp.int32, shape, 0)
    lane = lax.broadcasted_iota(jnp.int32, shape, 1)
    p = [[a_ref[r0 + 8 * g : r0 + 8 * g + 8, edge + 128 * u : edge + 128 * u + 128] for u in range(tiles)] for g in range(groups)]

    def column(v, m):
        return jnp.broadcast_to(v[:, m : m + 1], shape)

    def line(v, i):
        return jnp.broadcast_to(v[i : i + 1], shape)

    for k in range(groups):
        off = r0 - edge + 8 * k
        cols = {g: [column(p[g][0], off + m) for m in range(8)] for g in range(k, groups)}
        pivots = None
        for j in range(8):
            head = cols[k][j]
            pivot = line(head, j)
            across = {m: line(cols[k][m], j) for m in range(j + 1, 8)}
            rows = [line(p[k][u], j) for u in range(tiles)]
            inv = lax.rsqrt(pivot)
            inv2 = inv * inv
            pivots = inv if j == 0 else jnp.where(sub == j, inv, pivots)
            if j < 7:
                first = head * across[j + 1]
                cols[k][j + 1] = cols[k][j + 1] - first * inv2
                scaled = head * inv2
                for m in range(j + 2, 8):
                    cols[k][m] = cols[k][m] - scaled * across[m]
                below = jnp.where(sub > j, scaled, 0.0)
                for u in range(tiles):
                    p[k][u] = p[k][u] - below * rows[u]
            for g in range(k + 1, groups):
                scaled = cols[g][j] * inv2
                for m in range(j + 1, 8):
                    cols[g][m] = cols[g][m] - scaled * across[m]
                for u in range(tiles):
                    p[g][u] = p[g][u] - scaled * rows[u]
        for u in range(tiles):
            v = p[k][u] * pivots
            if u == 0:
                v = jnp.where(lane >= off + sub, v, 0.0)
            p[k][u] = v
            r_ref[r0 + 8 * k : r0 + 8 * k + 8, edge + 128 * u : edge + 128 * u + 128] = v * full
    rest = r0 + span
    if rest < order:
        start = rest // 128 * 128
        x = jnp.concatenate([jnp.concatenate(p[g][(start - edge) // 128 :], axis=1) for g in range(groups)], axis=0)
        high = x.astype(BF16)
        low = (x - high.astype(F32)).astype(BF16)
        update = dot(jnp.concatenate([high, high, low], axis=0), jnp.concatenate([high, low, high], axis=0), ((0,), (0,)))
        a_ref[rest:, start:] = a_ref[rest:, start:] - update[rest - start:]


def filter_response(replica_ref, gates, rim):
    taps = replica_ref.shape[1]
    lane = lax.broadcasted_iota(jnp.int32, (gates, gates), 1)
    row = lax.broadcasted_iota(jnp.int32, (gates, gates), 0)
    back = (gates - lane[:8]) % gates
    rolled = []
    for part in range(2):
        line = jnp.concatenate([replica_ref[part : part + 1], jnp.zeros((1, gates - taps), F32)], axis=1)
        line = jnp.take_along_axis(jnp.broadcast_to(line, (8, gates)), back, axis=1)
        rolled.append(pltpu.roll(jnp.broadcast_to(line[:1], (gates, gates)), 0, 1, stride=1, stride_axis=0))
    near = (row >= lane) & (row - lane < taps)
    far = (row[:rim] + gates - lane[:rim]) < taps
    re_near, im_near = [jnp.where(near, part, 0.0) for part in rolled]
    re_far, im_far = [jnp.where(far, part[:rim], 0.0) for part in rolled]
    return (
        jnp.concatenate(
            [jnp.concatenate([re_near, -im_near], axis=1), jnp.concatenate([im_near, re_near], axis=1)], axis=0
        ),
        jnp.concatenate(
            [jnp.concatenate([re_far, -im_far], axis=1), jnp.concatenate([im_far, re_far], axis=1)], axis=0
        ),
    )


def kernel(
    count_rows, sizes, counts_ref, replica_ref, raw_hbm, high_hbm, low_hbm, weights_hbm, pivots_hbm, gates_hbm, out_ref,
    raw_ref, high_ref, low_ref, weights_ref, pivots_ref, gates_ref,
    rim_out_ref, rim_in_ref, part_ref, spec_ref, pick_ref, starts_ref,
    pack_ref, recv_ref, bsend_ref, brecv_ref, a_ref, r_ref,
    load_sem, rim_send_sem, rim_recv_sem, send_sem, recv_sem, bsend_sem, brecv_sem, rsend_sem, rrecv_sem,
):
    ny, nz, nc, nx = sizes
    owners = ny * nz * nc
    _, channels, gates, pulses = raw_ref.shape
    rim = rim_in_ref.shape[2]
    most, wide = pack_ref.shape[1], pack_ref.shape[3]
    dop, rng = lax.axis_index("dop"), lax.axis_index("rng")
    y, z, c = dop // (nz * nc), (dop // nc) % nz, dop % nc
    tn = ((0,), (0,))

    def owner_at(ky, kz, kc):
        return (((y + ky) % ny) * nz + (z + kz) % nz) * nc + (c + kc) % nc

    loads = [
        pltpu.make_async_copy(raw_hbm.at[:, :, :rim], raw_ref.at[:, :, :rim], load_sem.at[0]),
        pltpu.make_async_copy(high_hbm, high_ref, load_sem.at[1]),
        pltpu.make_async_copy(low_hbm, low_ref, load_sem.at[2]),
        pltpu.make_async_copy(raw_hbm.at[:, :, rim:], raw_ref.at[:, :, rim:], load_sem.at[3]),
        pltpu.make_async_copy(gates_hbm, gates_ref, load_sem.at[4]),
        pltpu.make_async_copy(pivots_hbm, pivots_ref, load_sem.at[5]),
        pltpu.make_async_copy(weights_hbm, weights_ref, load_sem.at[6]),
    ]
    for load in loads:
        load.start()

    barrier = pltpu.get_barrier_semaphore()
    steps = [(ky, kz, kc) for ky in range(ny) for kz in range(nz) for kc in range(nc)][1:]
    for step in sorted(steps, key=lambda k: -min(k[0], ny - k[0]) - min(k[1], nz - k[1])):
        pl.semaphore_signal(barrier, inc=1, device_id=(owner_at(*step), rng), device_id_type=MESH)
    for k in range(1, nx):
        pl.semaphore_signal(barrier, inc=1, device_id=(dop, (rng + k) % nx), device_id_type=MESH)

    loads[0].wait()
    for ch in range(channels):
        for part in range(2):
            rim_out_ref[ch, part] = raw_ref[part, ch, :rim].astype(BF16)

    pl.semaphore_wait(barrier, owners - 1 + nx - 1)

    @pl.when(rng > 0)
    def _():
        for ch in range(channels):
            pltpu.make_async_remote_copy(
                src_ref=rim_out_ref.at[ch], dst_ref=rim_in_ref.at[ch], send_sem=rim_send_sem.at[ch],
                recv_sem=rim_recv_sem.at[ch], device_id=(dop, rng - 1), device_id_type=MESH,
            ).start()

    @pl.when(rng == nx - 1)
    def _():
        rim_in_ref[...] = jnp.zeros_like(rim_in_ref)

    near, far = filter_response(replica_ref, gates, rim)
    near_high, near_low = halves(near)
    far_high, far_low = halves(far)
    for load in loads[1:4]:
        load.wait()
    for ch in range(channels):
        high, low = halves(jnp.concatenate([raw_ref[0, ch], raw_ref[1, ch]], axis=1))
        inner = dot(high, high_ref[...]) + (dot(low, high_ref[...]) + dot(high, low_ref[...]))
        high, low = halves(jnp.concatenate([inner[:, :pulses], inner[:, pulses:]], axis=0))
        part_ref[ch] = dot(high, near_high, tn) + (dot(low, near_high, tn) + dot(high, near_low, tn))

    def run(owner, total):
        starts_ref[owner] = total
        return total + counts_ref[owner]

    lax.fori_loop(0, owners, run, 0)
    loads[4].wait()
    local = gates_ref[...].T % gates
    pick_ref[...] = jnp.concatenate([local, local], axis=1)

    for ch in range(channels):
        @pl.when(rng < nx - 1)
        def _():
            pltpu.make_async_copy(rim_in_ref.at[ch], rim_in_ref.at[ch], rim_recv_sem.at[ch]).wait()

        edge = jnp.concatenate([rim_in_ref[ch, 0], rim_in_ref[ch, 1]], axis=1)
        outer = dot(edge, high_ref[...]) + dot(edge, low_ref[...])
        high, low = halves(jnp.concatenate([outer[:, :pulses], outer[:, pulses:]], axis=0))
        done = dot(high, far_high, tn) + (dot(low, far_high, tn) + dot(high, far_low, tn))
        done = done + part_ref[ch]
        spec_ref[:, ch, :] = done[:, :gates]
        spec_ref[:, channels + ch, :] = done[:, gates:]

    first_half = lax.broadcasted_iota(jnp.int32, (channels, wide), 1) < wide // 2

    def pack(owner, ref):
        for slot in range(most):
            b = jnp.minimum(starts_ref[owner] + slot, pulses - 1)
            index = jnp.broadcast_to(pick_ref[pl.ds(b, 1), :], (channels, wide))
            real = jnp.take_along_axis(spec_ref[b, :channels], index, axis=1)
            imag = jnp.take_along_axis(spec_ref[b, channels:], index, axis=1)
            ref[owner, slot] = jnp.where(first_half, real, imag).astype(BF16)

    def send(owner):
        pltpu.make_async_remote_copy(
            src_ref=pack_ref.at[owner], dst_ref=recv_ref.at[dop], send_sem=send_sem, recv_sem=recv_sem,
            device_id=(owner, rng), device_id_type=MESH,
        ).start()

    steps = ny * nc
    for kz in sorted(range(nz), key=lambda k: (min(k, nz - k), k)):
        def at(i, kz=kz):
            return owner_at(i % ny, kz, i // ny)

        first = 0 if kz else 1
        pack(at(first), pack_ref)

        def one(i, carry):
            pack(at(i), pack_ref)
            send(at(i - 1))
            return carry

        lax.fori_loop(first + 1, steps, one, 0)
        send(at(steps - 1))
    pack(dop, recv_ref)

    loads[5].wait()
    loads[6].wait()
    dof = pivots_ref.shape[0]
    order = 2 * dof
    slot_bin = jnp.minimum(starts_ref[dop] + rng, pulses - 1)
    full = jnp.where(rng < counts_ref[dop], 1.0, 0.0)
    pivot = jnp.take_along_axis(pivots_ref[...], jnp.full(pivots_ref.shape, slot_bin, jnp.int32), axis=1)
    pivot = jnp.concatenate([pivot, pivot], axis=1)[:, :dof]
    chooser = (lax.broadcasted_iota(jnp.int32, (dof, dof), 1) == pivot).astype(BF16)
    r_ref[...] = jnp.zeros_like(r_ref)
    rows = order // nx
    for r in range(nx):
        first = (rows * r) // 128 * 128
        if first:
            @pl.when(rng == r)
            def _():
                out_ref[:, :, :first] = jnp.zeros((nx, rows, first), F32)

    others = recv_ref.at[pl.ds(0, owners - 1)]
    pltpu.make_async_copy(others, others, recv_sem).wait()

    sign = jnp.where(lax.broadcasted_iota(jnp.int32, (dof, wide), 1) < wide // 2, 1.0, -1.0)
    for k in range(1, nx + 1):
        slot = (rng + k) % nx
        data = recv_ref[:, slot].reshape(owners * channels, wide)
        beams = dot(weights_ref[0], data) + sign * pltpu.roll(dot(weights_ref[1], data), wide // 2, 1)
        if k < nx:
            bsend_ref[k - 1] = beams.astype(BF16)
            pltpu.make_async_remote_copy(
                src_ref=bsend_ref.at[k - 1], dst_ref=brecv_ref.at[rng], send_sem=bsend_sem.at[k - 1],
                recv_sem=brecv_sem.at[k - 1], device_id=(dop, slot), device_id_type=MESH,
            ).start()
        else:
            brecv_ref[rng] = beams.astype(BF16)
    for k in range(1, nx):
        pltpu.make_async_copy(bsend_ref.at[k - 1], bsend_ref.at[k - 1], brecv_sem.at[k - 1]).wait()

    parts = [dot(chooser, brecv_ref[k]) for k in range(nx)]
    upper = jnp.concatenate(parts, axis=1)
    lower = jnp.concatenate([sign * pltpu.roll(part, wide // 2, 1) for part in parts], axis=1)
    both = jnp.concatenate([upper, lower], axis=0).astype(BF16)
    gram = dot(both, both, ((1,), (1,)))
    diagonal = lax.broadcasted_iota(jnp.int32, (order, order), 0) == lax.broadcasted_iota(jnp.int32, (order, order), 1)
    a_ref[...] = gram * (1.0 / count_rows) + jnp.where(diagonal, LOADING, 0.0)

    def piece(r, ref):
        first = (rows * r) // 128 * 128
        return ref.at[:, first:] if first else ref

    def deliver(r):
        @pl.when(rng != r)
        def _():
            pltpu.make_async_remote_copy(
                src_ref=piece(r, r_ref.at[pl.ds(rows * r, rows)]), dst_ref=piece(r, out_ref.at[rng]),
                send_sem=rsend_sem.at[r], recv_sem=rrecv_sem.at[rng],
                device_id=(dop, r), device_id_type=MESH,
            ).start()

    span = 32
    for r0 in range(0, order, span):
        factor_rows(a_ref, r_ref, r0, full, span)
        if (r0 + span) % rows == 0:
            deliver((r0 + span) // rows - 1)

    pltpu.make_async_copy(others, others, send_sem).wait()
    for k in range(1, nx):
        pltpu.make_async_copy(bsend_ref.at[k - 1], bsend_ref.at[k - 1], bsend_sem.at[k - 1]).wait()

    @pl.when(rng > 0)
    def _():
        for ch in range(channels):
            pltpu.make_async_copy(rim_out_ref.at[ch], rim_out_ref.at[ch], rim_send_sem.at[ch]).wait()

    for r in range(nx):
        @pl.when(rng == r)
        def _():
            out_ref[r] = r_ref[rows * r : rows * r + rows]
            for s in range(nx):
                if s != r:
                    done = piece(r, out_ref.at[s])
                    pltpu.make_async_copy(done, done, rrecv_sem.at[s]).wait()

        @pl.when(rng != r)
        def _():
            left = piece(r, r_ref.at[pl.ds(rows * r, rows)])
            pltpu.make_async_copy(left, left, rsend_sem.at[r]).wait()


def local(sizes, raw_echo, replica, beam_weights, pivots, owner_counts, train_gates):
    _, channels, gates, pulses = raw_echo.shape
    taps = replica.shape[1]
    owners = owner_counts.shape[0]
    nx = sizes[3]
    dof = pivots.shape[1]
    order = 2 * dof
    chosen = train_gates.shape[1]
    most = 2 * (pulses // owners)
    count_rows = float(chosen * nx)
    high, low = doppler_table(pulses)
    weights, pivots, picks = beam_weights.transpose(0, 2, 1), pivots.T, train_gates.T
    vmem, anywhere = pl.BlockSpec(memory_space=pltpu.VMEM), pl.BlockSpec(memory_space=pl.ANY)
    dma = pltpu.SemaphoreType.DMA
    return pl.pallas_call(
        functools.partial(kernel, count_rows, sizes),
        out_shape=pltpu.VMEM((most, order // nx, order), F32),
        in_specs=[pl.BlockSpec(memory_space=pltpu.SMEM), vmem] + [anywhere] * 6,
        out_specs=vmem,
        scratch_shapes=[
            pltpu.VMEM(raw_echo.shape, F32),
            pltpu.VMEM(high.shape, BF16),
            pltpu.VMEM(low.shape, BF16),
            pltpu.VMEM(weights.shape, BF16),
            pltpu.VMEM(pivots.shape, jnp.int32),
            pltpu.VMEM(picks.shape, jnp.int32),
            pltpu.VMEM((channels, 2, taps, pulses), BF16),
            pltpu.VMEM((channels, 2, taps, pulses), BF16),
            pltpu.VMEM((channels, pulses, 2 * gates), F32),
            pltpu.VMEM((pulses, 2 * channels, gates), F32),
            pltpu.VMEM((pulses, 2 * chosen), jnp.int32),
            pltpu.SMEM((owners,), jnp.int32),
            pltpu.VMEM((owners, most, channels, 2 * chosen), BF16),
            pltpu.VMEM((owners, most, channels, 2 * chosen), BF16),
            pltpu.VMEM((nx - 1, dof, 2 * chosen), BF16),
            pltpu.VMEM((nx, dof, 2 * chosen), BF16),
            pltpu.VMEM((order, order), F32),
            pltpu.VMEM((order, order), F32),
            dma((7,)), dma((channels,)), dma((channels,)), dma, dma,
            dma((nx - 1,)), dma((nx - 1,)), dma((nx,)), dma((nx,)),
        ],
        compiler_params=pltpu.CompilerParams(collective_id=1, has_side_effects=True),
        name="factors",
    )(owner_counts, replica, raw_echo, jnp.asarray(high), jnp.asarray(low), weights, pivots, picks)


def solution(mesh):
    return jax.shard_map(
        functools.partial(local, (4, 8, 2, 4)),
        mesh=mesh,
        in_specs=(P(None, "dop", "rng", None), P(), P(), P(), P(), P(None, "rng")),
        out_specs=P("dop", "rng", None),
        check_vma=False,
    )
```

```python
import functools
import math

import jax
import jax.numpy as jnp
import numpy as np
from jax import lax
from jax.experimental import pallas as pl
from jax.experimental.pallas import tpu as pltpu
from jax.sharding import PartitionSpec as P

LOADING = 0.25
MESH = pl.DeviceIdType.MESH
BF16 = jnp.bfloat16
F32 = jnp.float32


def doppler_table(pulse_count):
    index = np.arange(pulse_count, dtype=np.int32)
    phase = (index[:, None] * index[None, :]) % pulse_count
    angle = phase.astype(np.float32) * np.float32(2.0 * math.pi / pulse_count)
    scale = np.float32(1.0 / math.sqrt(pulse_count))
    cos, sin = np.cos(angle) * scale, np.sin(angle) * scale
    table = np.block([[cos, -sin], [sin, cos]]).astype(np.float32)
    high = table.astype(BF16)
    low = (table - high.astype(np.float32)).astype(BF16)
    return high, low


def halves(x):
    high = x.astype(BF16)
    return high, (x - high.astype(F32)).astype(BF16)


def dot(a, b, dims=((1,), (0,))):
    return lax.dot_general(a, b, (dims, ((), ())), preferred_element_type=F32)


def factor_rows(a_ref, r_ref, r0, full, span):
    order = a_ref.shape[1]
    edge = r0 // 128 * 128
    tiles, groups = (order - edge) // 128, span // 8
    shape = (8, 128)
    sub = lax.broadcasted_iota(jnp.int32, shape, 0)
    lane = lax.broadcasted_iota(jnp.int32, shape, 1)
    p = [[a_ref[r0 + 8 * g : r0 + 8 * g + 8, edge + 128 * u : edge + 128 * u + 128] for u in range(tiles)] for g in range(groups)]

    def column(v, m):
        return jnp.broadcast_to(v[:, m : m + 1], shape)

    def line(v, i):
        return jnp.broadcast_to(v[i : i + 1], shape)

    for k in range(groups):
        off = r0 - edge + 8 * k
        cols = {g: [column(p[g][0], off + m) for m in range(8)] for g in range(k, groups)}
        pivots = None
        for j in range(8):
            head = cols[k][j]
            pivot = line(head, j)
            across = {m: line(cols[k][m], j) for m in range(j + 1, 8)}
            rows = [line(p[k][u], j) for u in range(tiles)]
            inv = lax.rsqrt(pivot)
            inv2 = inv * inv
            pivots = inv if j == 0 else jnp.where(sub == j, inv, pivots)
            if j < 7:
                first = head * across[j + 1]
                cols[k][j + 1] = cols[k][j + 1] - first * inv2
                scaled = head * inv2
                for m in range(j + 2, 8):
                    cols[k][m] = cols[k][m] - scaled * across[m]
                below = jnp.where(sub > j, scaled, 0.0)
                for u in range(tiles):
                    p[k][u] = p[k][u] - below * rows[u]
            for g in range(k + 1, groups):
                scaled = cols[g][j] * inv2
                for m in range(j + 1, 8):
                    cols[g][m] = cols[g][m] - scaled * across[m]
                for u in range(tiles):
                    p[g][u] = p[g][u] - scaled * rows[u]
        for u in range(tiles):
            v = p[k][u] * pivots
            if u == 0:
                v = jnp.where(lane >= off + sub, v, 0.0)
            p[k][u] = v
            r_ref[r0 + 8 * k : r0 + 8 * k + 8, edge + 128 * u : edge + 128 * u + 128] = v * full
    rest = r0 + span
    if rest < order:
        start = rest // 128 * 128
        x = jnp.concatenate([jnp.concatenate(p[g][(start - edge) // 128 :], axis=1) for g in range(groups)], axis=0)
        high = x.astype(BF16)
        low = (x - high.astype(F32)).astype(BF16)
        update = dot(jnp.concatenate([high, high, low], axis=0), jnp.concatenate([high, low, high], axis=0), ((0,), (0,)))
        a_ref[rest:, start:] = a_ref[rest:, start:] - update[rest - start:]


def filter_response(replica_ref, gates, rim):
    taps = replica_ref.shape[1]
    lane = lax.broadcasted_iota(jnp.int32, (gates, gates), 1)
    row = lax.broadcasted_iota(jnp.int32, (gates, gates), 0)
    back = (gates - lane[:8]) % gates
    rolled = []
    for part in range(2):
        line = jnp.concatenate([replica_ref[part : part + 1], jnp.zeros((1, gates - taps), F32)], axis=1)
        line = jnp.take_along_axis(jnp.broadcast_to(line, (8, gates)), back, axis=1)
        rolled.append(pltpu.roll(jnp.broadcast_to(line[:1], (gates, gates)), 0, 1, stride=1, stride_axis=0))
    near = (row >= lane) & (row - lane < taps)
    far = (row[:rim] + gates - lane[:rim]) < taps
    re_near, im_near = [jnp.where(near, part, 0.0) for part in rolled]
    re_far, im_far = [jnp.where(far, part[:rim], 0.0) for part in rolled]
    return (
        jnp.concatenate(
            [jnp.concatenate([re_near, -im_near], axis=1), jnp.concatenate([im_near, re_near], axis=1)], axis=0
        ),
        jnp.concatenate(
            [jnp.concatenate([re_far, -im_far], axis=1), jnp.concatenate([im_far, re_far], axis=1)], axis=0
        ),
    )


def kernel(
    count_rows, sizes, counts_ref, replica_ref, raw_hbm, high_hbm, low_hbm, weights_hbm, pivots_hbm, gates_hbm, out_ref,
    raw_ref, high_ref, low_ref, weights_ref, pivots_ref, gates_ref,
    rim_out_ref, rim_in_ref, part_ref, spec_ref, pick_ref, starts_ref,
    pack_ref, recv_ref, bsend_ref, brecv_ref, a_ref, r_ref,
    load_sem, rim_send_sem, rim_recv_sem, send_sem, recv_sem, bsend_sem, brecv_sem, rsend_sem, rrecv_sem, wave_sem,
):
    ny, nz, nc, nx = sizes
    owners = ny * nz * nc
    _, channels, gates, pulses = raw_ref.shape
    rim = rim_in_ref.shape[2]
    most, wide = pack_ref.shape[1], pack_ref.shape[3]
    dop, rng = lax.axis_index("dop"), lax.axis_index("rng")
    y, z, c = dop // (nz * nc), (dop // nc) % nz, dop % nc
    tn = ((0,), (0,))

    def owner_at(ky, kz, kc):
        return (((y + ky) % ny) * nz + (z + kz) % nz) * nc + (c + kc) % nc

    loads = [
        pltpu.make_async_copy(raw_hbm.at[:, :, :rim], raw_ref.at[:, :, :rim], load_sem.at[0]),
        pltpu.make_async_copy(high_hbm, high_ref, load_sem.at[1]),
        pltpu.make_async_copy(low_hbm, low_ref, load_sem.at[2]),
        pltpu.make_async_copy(raw_hbm.at[:, :, rim:], raw_ref.at[:, :, rim:], load_sem.at[3]),
        pltpu.make_async_copy(gates_hbm, gates_ref, load_sem.at[4]),
        pltpu.make_async_copy(pivots_hbm, pivots_ref, load_sem.at[5]),
        pltpu.make_async_copy(weights_hbm, weights_ref, load_sem.at[6]),
    ]
    for load in loads:
        load.start()

    barrier = pltpu.get_barrier_semaphore()
    along_y = [owner_at(k, 0, 0) for k in range(1, ny)]
    near = along_y + [owner_at(0, 1, 0), owner_at(0, nz - 1, 0), owner_at(0, 0, 1)]
    for other in near:
        pl.semaphore_signal(barrier, inc=1, device_id=(other, rng), device_id_type=MESH)
    for k in range(1, nx):
        pl.semaphore_signal(barrier, inc=1, device_id=(dop, (rng + k) % nx), device_id_type=MESH)
    waves = [
        [owner_at(0, 1, 0), owner_at(0, nz - 1, 0)],
        [owner_at(0, 2, 0), owner_at(0, nz - 2, 0)],
        along_y,
        [owner_at(0, 0, 1)],
    ]

    def wave(number):
        for other in waves[number]:
            pl.semaphore_signal(wave_sem.at[number], inc=1, device_id=(other, rng), device_id_type=MESH)

    def wave_end(number):
        pl.semaphore_wait(wave_sem.at[number], len(waves[number]))

    loads[0].wait()
    for ch in range(channels):
        for part in range(2):
            rim_out_ref[ch, part] = raw_ref[part, ch, :rim].astype(BF16)

    pl.semaphore_wait(barrier, len(near) + nx - 1)

    @pl.when(rng > 0)
    def _():
        for ch in range(channels):
            pltpu.make_async_remote_copy(
                src_ref=rim_out_ref.at[ch], dst_ref=rim_in_ref.at[ch], send_sem=rim_send_sem.at[ch],
                recv_sem=rim_recv_sem.at[ch], device_id=(dop, rng - 1), device_id_type=MESH,
            ).start()

    @pl.when(rng == nx - 1)
    def _():
        rim_in_ref[...] = jnp.zeros_like(rim_in_ref)

    wave(0)

    own, next_ = filter_response(replica_ref, gates, rim)
    near_high, near_low = halves(own)
    far_high, far_low = halves(next_)
    for load in loads[1:4]:
        load.wait()
    for ch in range(channels):
        high, low = halves(jnp.concatenate([raw_ref[0, ch], raw_ref[1, ch]], axis=1))
        inner = dot(high, high_ref[...]) + (dot(low, high_ref[...]) + dot(high, low_ref[...]))
        high, low = halves(jnp.concatenate([inner[:, :pulses], inner[:, pulses:]], axis=0))
        if ch < len(waves):
            wave_end(ch)
            if ch + 1 < len(waves):
                wave(ch + 1)
        part_ref[ch] = dot(high, near_high, tn) + (dot(low, near_high, tn) + dot(high, near_low, tn))

    def run(owner, total):
        starts_ref[owner] = total
        return total + counts_ref[owner]

    lax.fori_loop(0, owners, run, 0)
    loads[4].wait()
    local = gates_ref[...].T % gates
    pick_ref[...] = jnp.concatenate([local, local], axis=1)

    for ch in range(channels):
        @pl.when(rng < nx - 1)
        def _():
            pltpu.make_async_copy(rim_in_ref.at[ch], rim_in_ref.at[ch], rim_recv_sem.at[ch]).wait()

        edge = jnp.concatenate([rim_in_ref[ch, 0], rim_in_ref[ch, 1]], axis=1)
        outer = dot(edge, high_ref[...]) + dot(edge, low_ref[...])
        high, low = halves(jnp.concatenate([outer[:, :pulses], outer[:, pulses:]], axis=0))
        done = dot(high, far_high, tn) + (dot(low, far_high, tn) + dot(high, far_low, tn))
        done = done + part_ref[ch]
        spec_ref[:, ch, :] = done[:, :gates]
        spec_ref[:, channels + ch, :] = done[:, gates:]

    first_half = lax.broadcasted_iota(jnp.int32, (channels, wide), 1) < wide // 2

    def pack(owner, ref):
        for slot in range(most):
            b = jnp.minimum(starts_ref[owner] + slot, pulses - 1)
            index = jnp.broadcast_to(pick_ref[pl.ds(b, 1), :], (channels, wide))
            real = jnp.take_along_axis(spec_ref[b, :channels], index, axis=1)
            imag = jnp.take_along_axis(spec_ref[b, channels:], index, axis=1)
            ref[owner, slot] = jnp.where(first_half, real, imag).astype(BF16)

    def send(owner):
        pltpu.make_async_remote_copy(
            src_ref=pack_ref.at[owner], dst_ref=recv_ref.at[dop], send_sem=send_sem, recv_sem=recv_sem,
            device_id=(owner, rng), device_id_type=MESH,
        ).start()

    steps = ny * nc
    for kz in sorted(range(nz), key=lambda k: (min(k, nz - k), k)):
        def at(i, kz=kz):
            return owner_at(i % ny, kz, i // ny)

        first = 0 if kz else 1
        pack(at(first), pack_ref)

        def one(i, carry):
            pack(at(i), pack_ref)
            send(at(i - 1))
            return carry

        lax.fori_loop(first + 1, steps, one, 0)
        send(at(steps - 1))
    pack(dop, recv_ref)

    loads[5].wait()
    loads[6].wait()
    dof = pivots_ref.shape[0]
    order = 2 * dof
    slot_bin = jnp.minimum(starts_ref[dop] + rng, pulses - 1)
    full = jnp.where(rng < counts_ref[dop], 1.0, 0.0)
    pivot = jnp.take_along_axis(pivots_ref[...], jnp.full(pivots_ref.shape, slot_bin, jnp.int32), axis=1)
    pivot = jnp.concatenate([pivot, pivot], axis=1)[:, :dof]
    chooser = (lax.broadcasted_iota(jnp.int32, (dof, dof), 1) == pivot).astype(BF16)
    r_ref[...] = jnp.zeros_like(r_ref)
    rows = order // nx
    span = 32
    for r0 in range(0, order, span):
        first = r0 // 128 * 128
        if first:
            @pl.when(rng == r0 // rows)
            def _():
                out_ref[:, r0 % rows : r0 % rows + span, :first] = jnp.zeros((nx, span, first), F32)

    others = recv_ref.at[pl.ds(0, owners - 1)]
    pltpu.make_async_copy(others, others, recv_sem).wait()

    sign = jnp.where(lax.broadcasted_iota(jnp.int32, (dof, wide), 1) < wide // 2, 1.0, -1.0)
    for k in range(1, nx + 1):
        slot = (rng + k) % nx
        data = recv_ref[:, slot].reshape(owners * channels, wide)
        beams = dot(weights_ref[0], data) + sign * pltpu.roll(dot(weights_ref[1], data), wide // 2, 1)
        if k < nx:
            bsend_ref[k - 1] = beams.astype(BF16)
            pltpu.make_async_remote_copy(
                src_ref=bsend_ref.at[k - 1], dst_ref=brecv_ref.at[rng], send_sem=bsend_sem.at[k - 1],
                recv_sem=brecv_sem.at[k - 1], device_id=(dop, slot), device_id_type=MESH,
            ).start()
        else:
            brecv_ref[rng] = beams.astype(BF16)
    for k in range(1, nx):
        pltpu.make_async_copy(bsend_ref.at[k - 1], bsend_ref.at[k - 1], brecv_sem.at[k - 1]).wait()

    parts = [dot(chooser, brecv_ref[k]) for k in range(nx)]
    upper = jnp.concatenate(parts, axis=1)
    lower = jnp.concatenate([sign * pltpu.roll(part, wide // 2, 1) for part in parts], axis=1)
    both = jnp.concatenate([upper, lower], axis=0).astype(BF16)
    gram = dot(both, both, ((1,), (1,)))
    diagonal = lax.broadcasted_iota(jnp.int32, (order, order), 0) == lax.broadcasted_iota(jnp.int32, (order, order), 1)
    a_ref[...] = gram * (1.0 / count_rows) + jnp.where(diagonal, LOADING, 0.0)

    def source(r0):
        return r_ref.at[r0 : r0 + span, r0 // 128 * 128 :]

    def target(slot, r0):
        return out_ref.at[slot, r0 % rows : r0 % rows + span, r0 // 128 * 128 :]

    for r0 in range(0, order, span):
        factor_rows(a_ref, r_ref, r0, full, span)

        @pl.when(rng != r0 // rows)
        def _():
            pltpu.make_async_remote_copy(
                src_ref=source(r0), dst_ref=target(rng, r0), send_sem=rsend_sem.at[r0 // span],
                recv_sem=rrecv_sem.at[rng, r0 % rows // span], device_id=(dop, r0 // rows), device_id_type=MESH,
            ).start()

    pltpu.make_async_copy(others, others, send_sem).wait()
    for k in range(1, nx):
        pltpu.make_async_copy(bsend_ref.at[k - 1], bsend_ref.at[k - 1], bsend_sem.at[k - 1]).wait()

    @pl.when(rng > 0)
    def _():
        for ch in range(channels):
            pltpu.make_async_copy(rim_out_ref.at[ch], rim_out_ref.at[ch], rim_send_sem.at[ch]).wait()

    for r in range(nx):
        @pl.when(rng == r)
        def _():
            out_ref[r] = r_ref[rows * r : rows * r + rows]
            for r0 in range(rows * r, rows * r + rows, span):
                for slot in range(nx):
                    if slot != r:
                        done = target(slot, r0)
                        pltpu.make_async_copy(done, done, rrecv_sem.at[slot, r0 % rows // span]).wait()

        @pl.when(rng != r)
        def _():
            for r0 in range(rows * r, rows * r + rows, span):
                pltpu.make_async_copy(source(r0), source(r0), rsend_sem.at[r0 // span]).wait()


def local(sizes, raw_echo, replica, beam_weights, pivots, owner_counts, train_gates):
    _, channels, gates, pulses = raw_echo.shape
    taps = replica.shape[1]
    owners = owner_counts.shape[0]
    nx = sizes[3]
    dof = pivots.shape[1]
    order = 2 * dof
    chosen = train_gates.shape[1]
    most = 2 * (pulses // owners)
    count_rows = float(chosen * nx)
    high, low = doppler_table(pulses)
    weights, pivots, picks = beam_weights.transpose(0, 2, 1), pivots.T, train_gates.T
    vmem, anywhere = pl.BlockSpec(memory_space=pltpu.VMEM), pl.BlockSpec(memory_space=pl.ANY)
    dma = pltpu.SemaphoreType.DMA
    return pl.pallas_call(
        functools.partial(kernel, count_rows, sizes),
        out_shape=pltpu.VMEM((most, order // nx, order), F32),
        in_specs=[pl.BlockSpec(memory_space=pltpu.SMEM), vmem] + [anywhere] * 6,
        out_specs=vmem,
        scratch_shapes=[
            pltpu.VMEM(raw_echo.shape, F32),
            pltpu.VMEM(high.shape, BF16),
            pltpu.VMEM(low.shape, BF16),
            pltpu.VMEM(weights.shape, BF16),
            pltpu.VMEM(pivots.shape, jnp.int32),
            pltpu.VMEM(picks.shape, jnp.int32),
            pltpu.VMEM((channels, 2, taps, pulses), BF16),
            pltpu.VMEM((channels, 2, taps, pulses), BF16),
            pltpu.VMEM((channels, pulses, 2 * gates), F32),
            pltpu.VMEM((pulses, 2 * channels, gates), F32),
            pltpu.VMEM((pulses, 2 * chosen), jnp.int32),
            pltpu.SMEM((owners,), jnp.int32),
            pltpu.VMEM((owners, most, channels, 2 * chosen), BF16),
            pltpu.VMEM((owners, most, channels, 2 * chosen), BF16),
            pltpu.VMEM((nx - 1, dof, 2 * chosen), BF16),
            pltpu.VMEM((nx, dof, 2 * chosen), BF16),
            pltpu.VMEM((order, order), F32),
            pltpu.VMEM((order, order), F32),
            dma((7,)), dma((channels,)), dma((channels,)), dma, dma,
            dma((nx - 1,)), dma((nx - 1,)), dma((order // 32,)), dma((nx, order // nx // 32)),
            pltpu.SemaphoreType.REGULAR((4,)),
        ],
        compiler_params=pltpu.CompilerParams(collective_id=1, has_side_effects=True),
        name="factors",
    )(owner_counts, replica, raw_echo, jnp.asarray(high), jnp.asarray(low), weights, pivots, picks)


def solution(mesh):
    return jax.shard_map(
        functools.partial(local, (4, 8, 2, 4)),
        mesh=mesh,
        in_specs=(P(None, "dop", "rng", None), P(), P(), P(), P(), P(None, "rng")),
        out_specs=P("dop", "rng", None),
        check_vma=False,
    )
```

```python
import functools
import math

import jax
import jax.numpy as jnp
import numpy as np
from jax import lax
from jax.experimental import pallas as pl
from jax.experimental.pallas import tpu as pltpu
from jax.sharding import PartitionSpec as P

LOADING = 0.25
MESH = pl.DeviceIdType.MESH
BF16 = jnp.bfloat16
F32 = jnp.float32


def doppler_table(pulse_count):
    index = np.arange(pulse_count, dtype=np.int32)
    phase = (index[:, None] * index[None, :]) % pulse_count
    angle = phase.astype(np.float32) * np.float32(2.0 * math.pi / pulse_count)
    scale = np.float32(1.0 / math.sqrt(pulse_count))
    cos, sin = np.cos(angle) * scale, np.sin(angle) * scale
    table = np.block([[cos, -sin], [sin, cos]]).astype(np.float32)
    high = table.astype(BF16)
    low = (table - high.astype(np.float32)).astype(BF16)
    return high, low


def halves(x):
    high = x.astype(BF16)
    return high, (x - high.astype(F32)).astype(BF16)


def dot(a, b, dims=((1,), (0,))):
    return lax.dot_general(a, b, (dims, ((), ())), preferred_element_type=F32)


def factor_rows(a_ref, r_ref, r0, full, span):
    order = a_ref.shape[1]
    edge = r0 // 128 * 128
    tiles, groups = (order - edge) // 128, span // 8
    shape = (8, 128)
    sub = lax.broadcasted_iota(jnp.int32, shape, 0)
    lane = lax.broadcasted_iota(jnp.int32, shape, 1)
    p = [[a_ref[r0 + 8 * g : r0 + 8 * g + 8, edge + 128 * u : edge + 128 * u + 128] for u in range(tiles)] for g in range(groups)]

    def column(v, m):
        return jnp.take_along_axis(v, jnp.full(shape, m, jnp.int32), axis=1)

    def line(v, i):
        return jnp.broadcast_to(v[i : i + 1], shape)

    for k in range(groups):
        off = r0 - edge + 8 * k
        cols = {g: [column(p[g][0], off + m) for m in range(8)] for g in range(k + 1, groups)}
        cols[k] = ahead if k else [column(p[k][0], off + m) for m in range(8)]
        if k + 1 < groups:
            ahead = [column(p[k + 1][0], off + 8 + m) for m in range(8)]
        pivots = None
        for j in range(8):
            head = cols[k][j]
            pivot = line(head, j)
            across = {m: line(cols[k][m], j) for m in range(j + 1, 8)}
            rows = [line(p[k][u], j) for u in range(tiles)]
            inv = lax.rsqrt(pivot)
            inv2 = inv * inv
            pivots = inv if j == 0 else jnp.where(sub == j, inv, pivots)
            if j < 7:
                first = head * across[j + 1]
                cols[k][j + 1] = cols[k][j + 1] - first * inv2
                scaled = head * inv2
                for m in range(j + 2, 8):
                    cols[k][m] = cols[k][m] - scaled * across[m]
                below = jnp.where(sub > j, scaled, 0.0)
                for u in range(tiles):
                    p[k][u] = p[k][u] - below * rows[u]
            for g in range(k + 1, groups):
                scaled = cols[g][j] * inv2
                if g == k + 1:
                    for m in range(8):
                        ahead[m] = ahead[m] - scaled * line(cols[g][j], m)
                for m in range(j + 1, 8):
                    cols[g][m] = cols[g][m] - scaled * across[m]
                for u in range(tiles):
                    p[g][u] = p[g][u] - scaled * rows[u]
        for u in range(tiles):
            v = p[k][u] * pivots
            if u == 0:
                v = jnp.where(lane >= off + sub, v, 0.0)
            p[k][u] = v
            r_ref[r0 + 8 * k : r0 + 8 * k + 8, edge + 128 * u : edge + 128 * u + 128] = v * full
    rest = r0 + span
    if rest < order:
        start = rest // 128 * 128
        x = jnp.concatenate([jnp.concatenate(p[g][(start - edge) // 128 :], axis=1) for g in range(groups)], axis=0)
        high = x.astype(BF16)
        low = (x - high.astype(F32)).astype(BF16)
        update = dot(jnp.concatenate([high, high, low], axis=0), jnp.concatenate([high, low, high], axis=0), ((0,), (0,)))
        a_ref[rest:, start:] = a_ref[rest:, start:] - update[rest - start:]


def filter_response(replica_ref, gates, rim):
    taps = replica_ref.shape[1]
    lane = lax.broadcasted_iota(jnp.int32, (gates, gates), 1)
    row = lax.broadcasted_iota(jnp.int32, (gates, gates), 0)
    back = (gates - lane[:8]) % gates
    rolled = []
    for part in range(2):
        line = jnp.concatenate([replica_ref[part : part + 1], jnp.zeros((1, gates - taps), F32)], axis=1)
        line = jnp.take_along_axis(jnp.broadcast_to(line, (8, gates)), back, axis=1)
        rolled.append(pltpu.roll(jnp.broadcast_to(line[:1], (gates, gates)), 0, 1, stride=1, stride_axis=0))
    near = (row >= lane) & (row - lane < taps)
    far = (row[:rim] + gates - lane[:rim]) < taps
    re_near, im_near = [jnp.where(near, part, 0.0) for part in rolled]
    re_far, im_far = [jnp.where(far, part[:rim], 0.0) for part in rolled]
    return (
        jnp.concatenate(
            [jnp.concatenate([re_near, -im_near], axis=1), jnp.concatenate([im_near, re_near], axis=1)], axis=0
        ),
        jnp.concatenate(
            [jnp.concatenate([re_far, -im_far], axis=1), jnp.concatenate([im_far, re_far], axis=1)], axis=0
        ),
    )


def kernel(
    count_rows, sizes, counts_ref, replica_ref, raw_hbm, high_hbm, low_hbm, weights_hbm, pivots_hbm, gates_hbm, out_ref,
    raw_ref, high_ref, low_ref, weights_ref, pivots_ref, gates_ref,
    rim_out_ref, rim_in_ref, part_ref, spec_ref, pick_ref, starts_ref,
    pack_ref, recv_ref, bsend_ref, brecv_ref, a_ref, r_ref,
    load_sem, rim_send_sem, rim_recv_sem, send_sem, recv_sem, bsend_sem, brecv_sem, rsend_sem, rrecv_sem, wave_sem,
):
    ny, nz, nc, nx = sizes
    owners = ny * nz * nc
    _, channels, gates, pulses = raw_ref.shape
    rim = rim_in_ref.shape[2]
    most, wide = pack_ref.shape[1], pack_ref.shape[3]
    dop, rng = lax.axis_index("dop"), lax.axis_index("rng")
    y, z, c = dop // (nz * nc), (dop // nc) % nz, dop % nc
    tn = ((0,), (0,))

    def owner_at(ky, kz, kc):
        return (((y + ky) % ny) * nz + (z + kz) % nz) * nc + (c + kc) % nc

    loads = [
        pltpu.make_async_copy(raw_hbm.at[:, :, :rim], raw_ref.at[:, :, :rim], load_sem.at[0]),
        pltpu.make_async_copy(high_hbm, high_ref, load_sem.at[1]),
        pltpu.make_async_copy(low_hbm, low_ref, load_sem.at[2]),
        pltpu.make_async_copy(raw_hbm.at[:, :, rim:], raw_ref.at[:, :, rim:], load_sem.at[3]),
        pltpu.make_async_copy(gates_hbm, gates_ref, load_sem.at[4]),
        pltpu.make_async_copy(pivots_hbm, pivots_ref, load_sem.at[5]),
        pltpu.make_async_copy(weights_hbm, weights_ref, load_sem.at[6]),
    ]
    for load in loads:
        load.start()

    barrier = pltpu.get_barrier_semaphore()
    along_y = [owner_at(k, 0, 0) for k in range(1, ny)]
    near = along_y + [owner_at(0, 1, 0), owner_at(0, nz - 1, 0), owner_at(0, 0, 1)]
    for other in near:
        pl.semaphore_signal(barrier, inc=1, device_id=(other, rng), device_id_type=MESH)
    for k in range(1, nx):
        pl.semaphore_signal(barrier, inc=1, device_id=(dop, (rng + k) % nx), device_id_type=MESH)
    waves = [
        [owner_at(0, 1, 0), owner_at(0, nz - 1, 0)],
        [owner_at(0, 2, 0), owner_at(0, nz - 2, 0)],
        along_y,
        [owner_at(0, 0, 1)],
    ]

    def wave(number):
        for other in waves[number]:
            pl.semaphore_signal(wave_sem.at[number], inc=1, device_id=(other, rng), device_id_type=MESH)

    def wave_end(number):
        pl.semaphore_wait(wave_sem.at[number], len(waves[number]))

    loads[0].wait()
    for ch in range(channels):
        for part in range(2):
            rim_out_ref[ch, part] = raw_ref[part, ch, :rim].astype(BF16)

    pl.semaphore_wait(barrier, len(near) + nx - 1)

    @pl.when(rng > 0)
    def _():
        for ch in range(channels):
            pltpu.make_async_remote_copy(
                src_ref=rim_out_ref.at[ch], dst_ref=rim_in_ref.at[ch], send_sem=rim_send_sem.at[ch],
                recv_sem=rim_recv_sem.at[ch], device_id=(dop, rng - 1), device_id_type=MESH,
            ).start()

    @pl.when(rng == nx - 1)
    def _():
        rim_in_ref[...] = jnp.zeros_like(rim_in_ref)

    wave(0)

    own, next_ = filter_response(replica_ref, gates, rim)
    near_high, near_low = halves(own)
    far_high, far_low = halves(next_)
    for load in loads[1:4]:
        load.wait()
    for ch in range(channels):
        high, low = halves(jnp.concatenate([raw_ref[0, ch], raw_ref[1, ch]], axis=1))
        inner = dot(high, high_ref[...]) + (dot(low, high_ref[...]) + dot(high, low_ref[...]))
        high, low = halves(jnp.concatenate([inner[:, :pulses], inner[:, pulses:]], axis=0))
        part_ref[ch] = dot(high, near_high, tn) + (dot(low, near_high, tn) + dot(high, near_low, tn))

    def run(owner, total):
        starts_ref[owner] = total
        return total + counts_ref[owner]

    lax.fori_loop(0, owners, run, 0)
    loads[4].wait()
    local = gates_ref[...].T % gates
    pick_ref[...] = jnp.concatenate([local, local], axis=1)

    wave_end(0)
    wave(1)

    for ch in range(channels):
        if ch in (2, 4, 6):
            wave_end(ch // 2)
            if ch < 6:
                wave(ch // 2 + 1)
        @pl.when(rng < nx - 1)
        def _():
            pltpu.make_async_copy(rim_in_ref.at[ch], rim_in_ref.at[ch], rim_recv_sem.at[ch]).wait()

        edge = jnp.concatenate([rim_in_ref[ch, 0], rim_in_ref[ch, 1]], axis=1)
        outer = dot(edge, high_ref[...]) + dot(edge, low_ref[...])
        high, low = halves(jnp.concatenate([outer[:, :pulses], outer[:, pulses:]], axis=0))
        done = dot(high, far_high, tn) + (dot(low, far_high, tn) + dot(high, far_low, tn))
        done = done + part_ref[ch]
        spec_ref[:, ch, :] = done[:, :gates]
        spec_ref[:, channels + ch, :] = done[:, gates:]

    first_half = lax.broadcasted_iota(jnp.int32, (channels, wide), 1) < wide // 2

    def pack(owner, ref):
        for slot in range(most):
            b = jnp.minimum(starts_ref[owner] + slot, pulses - 1)
            index = jnp.broadcast_to(pick_ref[pl.ds(b, 1), :], (channels, wide))
            real = jnp.take_along_axis(spec_ref[b, :channels], index, axis=1)
            imag = jnp.take_along_axis(spec_ref[b, channels:], index, axis=1)
            ref[owner, slot] = jnp.where(first_half, real, imag).astype(BF16)

    def send(owner):
        pltpu.make_async_remote_copy(
            src_ref=pack_ref.at[owner], dst_ref=recv_ref.at[dop], send_sem=send_sem, recv_sem=recv_sem,
            device_id=(owner, rng), device_id_type=MESH,
        ).start()

    steps = ny * nc
    for kz in sorted(range(nz), key=lambda k: (min(k, nz - k), k)):
        def at(i, kz=kz):
            return owner_at(i % ny, kz, i // ny)

        first = 0 if kz else 1
        pack(at(first), pack_ref)

        def one(i, carry):
            pack(at(i), pack_ref)
            send(at(i - 1))
            return carry

        lax.fori_loop(first + 1, steps, one, 0)
        send(at(steps - 1))
    pack(dop, recv_ref)

    loads[5].wait()
    loads[6].wait()
    dof = pivots_ref.shape[0]
    order = 2 * dof
    slot_bin = jnp.minimum(starts_ref[dop] + rng, pulses - 1)
    full = jnp.where(rng < counts_ref[dop], 1.0, 0.0)
    pivot = jnp.take_along_axis(pivots_ref[...], jnp.full(pivots_ref.shape, slot_bin, jnp.int32), axis=1)
    pivot = jnp.concatenate([pivot, pivot], axis=1)[:, :dof]
    chooser = (lax.broadcasted_iota(jnp.int32, (dof, dof), 1) == pivot).astype(BF16)
    r_ref[...] = jnp.zeros_like(r_ref)
    rows = order // nx
    span = 32
    last = order - rows
    pieces = [(lo, lo + rows) for lo in range(0, last, rows)] + [(lo, lo + span) for lo in range(last, order, span)]
    for lo, hi in pieces:
        first = lo // 128 * 128
        if first:
            @pl.when(rng == lo // rows)
            def _():
                out_ref[:, lo % rows : lo % rows + hi - lo, :first] = jnp.zeros((nx, hi - lo, first), F32)

    others = recv_ref.at[pl.ds(0, owners - 1)]
    pltpu.make_async_copy(others, others, recv_sem).wait()

    sign = jnp.where(lax.broadcasted_iota(jnp.int32, (dof, wide), 1) < wide // 2, 1.0, -1.0)
    for k in range(1, nx + 1):
        slot = (rng + k) % nx
        data = recv_ref[:, slot].reshape(owners * channels, wide)
        both = dot(weights_ref[...], data)
        beams = both[:dof] + sign * pltpu.roll(both[dof:], wide // 2, 1)
        if k < nx:
            bsend_ref[k - 1] = beams.astype(BF16)
            pltpu.make_async_remote_copy(
                src_ref=bsend_ref.at[k - 1], dst_ref=brecv_ref.at[rng], send_sem=bsend_sem.at[k - 1],
                recv_sem=brecv_sem.at[k - 1], device_id=(dop, slot), device_id_type=MESH,
            ).start()
        else:
            brecv_ref[rng] = beams.astype(BF16)
    for k in range(1, nx):
        pltpu.make_async_copy(bsend_ref.at[k - 1], bsend_ref.at[k - 1], brecv_sem.at[k - 1]).wait()

    parts = [dot(chooser, brecv_ref[k]) for k in range(nx)]
    upper = jnp.concatenate(parts, axis=1)
    lower = jnp.concatenate([sign * pltpu.roll(part, wide // 2, 1) for part in parts], axis=1)
    both = jnp.concatenate([upper, lower], axis=0).astype(BF16)
    gram = dot(both, both, ((1,), (1,)))
    diagonal = lax.broadcasted_iota(jnp.int32, (order, order), 0) == lax.broadcasted_iota(jnp.int32, (order, order), 1)
    a_ref[...] = gram * (1.0 / count_rows) + jnp.where(diagonal, LOADING, 0.0)

    def source(lo, hi):
        return r_ref.at[lo:hi, lo // 128 * 128 :]

    def target(slot, lo, hi):
        return out_ref.at[slot, lo % rows : lo % rows + hi - lo, lo // 128 * 128 :]

    for r0 in range(0, order, span):
        factor_rows(a_ref, r_ref, r0, full, span)
        for number, (lo, hi) in enumerate(pieces):
            if hi == r0 + span:
                @pl.when(rng != lo // rows)
                def _():
                    pltpu.make_async_remote_copy(
                        src_ref=source(lo, hi), dst_ref=target(rng, lo, hi), send_sem=rsend_sem.at[number],
                        recv_sem=rrecv_sem.at[rng, lo % rows // span], device_id=(dop, lo // rows), device_id_type=MESH,
                    ).start()

    pltpu.make_async_copy(others, others, send_sem).wait()
    for k in range(1, nx):
        pltpu.make_async_copy(bsend_ref.at[k - 1], bsend_ref.at[k - 1], bsend_sem.at[k - 1]).wait()

    @pl.when(rng > 0)
    def _():
        for ch in range(channels):
            pltpu.make_async_copy(rim_out_ref.at[ch], rim_out_ref.at[ch], rim_send_sem.at[ch]).wait()

    for r in range(nx):
        @pl.when(rng == r)
        def _():
            out_ref[r] = r_ref[rows * r : rows * r + rows]

    for number, (lo, hi) in enumerate(pieces):
        @pl.when(rng == lo // rows)
        def _():
            for slot in range(nx):
                if slot != lo // rows:
                    done = target(slot, lo, hi)
                    pltpu.make_async_copy(done, done, rrecv_sem.at[slot, lo % rows // span]).wait()

        @pl.when(rng != lo // rows)
        def _():
            pltpu.make_async_copy(source(lo, hi), source(lo, hi), rsend_sem.at[number]).wait()


def local(sizes, raw_echo, replica, beam_weights, pivots, owner_counts, train_gates):
    _, channels, gates, pulses = raw_echo.shape
    taps = replica.shape[1]
    owners = owner_counts.shape[0]
    nx = sizes[3]
    dof = pivots.shape[1]
    order = 2 * dof
    chosen = train_gates.shape[1]
    most = 2 * (pulses // owners)
    count_rows = float(chosen * nx)
    high, low = doppler_table(pulses)
    weights = beam_weights.transpose(0, 2, 1).reshape(order, -1)
    pivots, picks = pivots.T, train_gates.T
    vmem, anywhere = pl.BlockSpec(memory_space=pltpu.VMEM), pl.BlockSpec(memory_space=pl.ANY)
    dma = pltpu.SemaphoreType.DMA
    return pl.pallas_call(
        functools.partial(kernel, count_rows, sizes),
        out_shape=pltpu.VMEM((most, order // nx, order), F32),
        in_specs=[pl.BlockSpec(memory_space=pltpu.SMEM), vmem] + [anywhere] * 6,
        out_specs=vmem,
        scratch_shapes=[
            pltpu.VMEM(raw_echo.shape, F32),
            pltpu.VMEM(high.shape, BF16),
            pltpu.VMEM(low.shape, BF16),
            pltpu.VMEM(weights.shape, BF16),
            pltpu.VMEM(pivots.shape, jnp.int32),
            pltpu.VMEM(picks.shape, jnp.int32),
            pltpu.VMEM((channels, 2, taps, pulses), BF16),
            pltpu.VMEM((channels, 2, taps, pulses), BF16),
            pltpu.VMEM((channels, pulses, 2 * gates), F32),
            pltpu.VMEM((pulses, 2 * channels, gates), F32),
            pltpu.VMEM((pulses, 2 * chosen), jnp.int32),
            pltpu.SMEM((owners,), jnp.int32),
            pltpu.VMEM((owners, most, channels, 2 * chosen), BF16),
            pltpu.VMEM((owners, most, channels, 2 * chosen), BF16),
            pltpu.VMEM((nx - 1, dof, 2 * chosen), BF16),
            pltpu.VMEM((nx, dof, 2 * chosen), BF16),
            pltpu.VMEM((order, order), F32),
            pltpu.VMEM((order, order), F32),
            dma((7,)), dma((channels,)), dma((channels,)), dma, dma,
            dma((nx - 1,)), dma((nx - 1,)), dma((order // 32,)), dma((nx, order // nx // 32)),
            pltpu.SemaphoreType.REGULAR((4,)),
        ],
        compiler_params=pltpu.CompilerParams(collective_id=1, has_side_effects=True),
        name="factors",
    )(owner_counts, replica, raw_echo, jnp.asarray(high), jnp.asarray(low), weights, pivots, picks)


def solution(mesh):
    return jax.shard_map(
        functools.partial(local, (4, 8, 2, 4)),
        mesh=mesh,
        in_specs=(P(None, "dop", "rng", None), P(), P(), P(), P(), P(None, "rng")),
        out_specs=P("dop", "rng", None),
        check_vma=False,
    )
```

```python
import functools
import math

import jax
import jax.numpy as jnp
import numpy as np
from jax import lax
from jax.experimental import pallas as pl
from jax.experimental.pallas import tpu as pltpu
from jax.sharding import PartitionSpec as P

LOADING = 0.25
MESH = pl.DeviceIdType.MESH
BF16 = jnp.bfloat16
F32 = jnp.float32


def doppler_table(pulse_count):
    index = np.arange(pulse_count, dtype=np.int32)
    phase = (index[:, None] * index[None, :]) % pulse_count
    angle = phase.astype(np.float32) * np.float32(2.0 * math.pi / pulse_count)
    scale = np.float32(1.0 / math.sqrt(pulse_count))
    cos, sin = np.cos(angle) * scale, np.sin(angle) * scale
    table = np.block([[cos, -sin], [sin, cos]]).astype(np.float32)
    high = table.astype(BF16)
    low = (table - high.astype(np.float32)).astype(BF16)
    return high, low


def halves(x):
    high = x.astype(BF16)
    return high, (x - high.astype(F32)).astype(BF16)


def dot(a, b, dims=((1,), (0,))):
    return lax.dot_general(a, b, (dims, ((), ())), preferred_element_type=F32)


def factor_rows(a_ref, r_ref, r0, full, span):
    order = a_ref.shape[1]
    edge = r0 // 128 * 128
    tiles, groups = (order - edge) // 128, span // 8
    shape = (8, 128)
    sub = lax.broadcasted_iota(jnp.int32, shape, 0)
    lane = lax.broadcasted_iota(jnp.int32, shape, 1)
    p = [[a_ref[r0 + 8 * g : r0 + 8 * g + 8, edge + 128 * u : edge + 128 * u + 128] for u in range(tiles)] for g in range(groups)]

    def column(v, m):
        return jnp.take_along_axis(v, jnp.full(shape, m, jnp.int32), axis=1)

    def line(v, i):
        return jnp.broadcast_to(v[i : i + 1], shape)

    for k in range(groups):
        off = r0 - edge + 8 * k
        cols = {g: [column(p[g][0], off + m) for m in range(8)] for g in range(k + 1, groups)}
        cols[k] = ahead if k else [column(p[k][0], off + m) for m in range(8)]
        if k + 1 < groups:
            ahead = [column(p[k + 1][0], off + 8 + m) for m in range(8)]
        pivots = None
        for j in range(8):
            head = cols[k][j]
            pivot = line(head, j)
            across = {m: line(cols[k][m], j) for m in range(j + 1, 8)}
            rows = [line(p[k][u], j) for u in range(tiles)]
            inv = lax.rsqrt(pivot)
            inv2 = inv * inv
            pivots = inv if j == 0 else jnp.where(sub == j, inv, pivots)
            if j < 7:
                first = head * across[j + 1]
                cols[k][j + 1] = cols[k][j + 1] - first * inv2
                scaled = head * inv2
                for m in range(j + 2, 8):
                    cols[k][m] = cols[k][m] - scaled * across[m]
                below = jnp.where(sub > j, scaled, 0.0)
                for u in range(tiles):
                    p[k][u] = p[k][u] - below * rows[u]
            for g in range(k + 1, groups):
                scaled = cols[g][j] * inv2
                if g == k + 1:
                    for m in range(8):
                        ahead[m] = ahead[m] - scaled * line(cols[g][j], m)
                for m in range(j + 1, 8):
                    cols[g][m] = cols[g][m] - scaled * across[m]
                for u in range(tiles):
                    p[g][u] = p[g][u] - scaled * rows[u]
        for u in range(tiles):
            v = p[k][u] * pivots
            if u == 0:
                v = jnp.where(lane >= off + sub, v, 0.0)
            p[k][u] = v
            r_ref[r0 + 8 * k : r0 + 8 * k + 8, edge + 128 * u : edge + 128 * u + 128] = v * full
    rest = r0 + span
    if rest < order:
        start = rest // 128 * 128
        x = jnp.concatenate([jnp.concatenate(p[g][(start - edge) // 128 :], axis=1) for g in range(groups)], axis=0)
        high = x.astype(BF16)
        low = (x - high.astype(F32)).astype(BF16)
        update = dot(jnp.concatenate([high, high, low], axis=0), jnp.concatenate([high, low, high], axis=0), ((0,), (0,)))
        a_ref[rest:, start:] = a_ref[rest:, start:] - update[rest - start:]


def filter_response(replica_ref, gates, rim):
    taps = replica_ref.shape[1]
    lane = lax.broadcasted_iota(jnp.int32, (gates, gates), 1)
    row = lax.broadcasted_iota(jnp.int32, (gates, gates), 0)
    back = (gates - lane[:8]) % gates
    rolled = []
    for part in range(2):
        line = jnp.concatenate([replica_ref[part : part + 1], jnp.zeros((1, gates - taps), F32)], axis=1)
        line = jnp.take_along_axis(jnp.broadcast_to(line, (8, gates)), back, axis=1)
        rolled.append(pltpu.roll(jnp.broadcast_to(line[:1], (gates, gates)), 0, 1, stride=1, stride_axis=0))
    near = (row >= lane) & (row - lane < taps)
    far = (row[:rim] + gates - lane[:rim]) < taps
    re_near, im_near = [jnp.where(near, part, 0.0) for part in rolled]
    re_far, im_far = [jnp.where(far, part[:rim], 0.0) for part in rolled]
    return (
        jnp.concatenate(
            [jnp.concatenate([re_near, -im_near], axis=1), jnp.concatenate([im_near, re_near], axis=1)], axis=0
        ),
        jnp.concatenate(
            [jnp.concatenate([re_far, -im_far], axis=1), jnp.concatenate([im_far, re_far], axis=1)], axis=0
        ),
    )


def kernel(
    count_rows, sizes, counts_ref, replica_ref, raw_hbm, high_hbm, low_hbm, weights_hbm, pivots_hbm, gates_hbm, out_ref,
    raw_ref, high_ref, low_ref, weights_ref, pivots_ref, gates_ref,
    rim_out_ref, rim_in_ref, part_ref, spec_ref, pick_ref, starts_ref,
    mixed_ref, pack_ref, recv_ref, bsend_ref, brecv_ref, a_ref, r_ref,
    load_sem, rim_send_sem, rim_recv_sem, send_sem, recv_sem, bsend_sem, brecv_sem, rsend_sem, rrecv_sem, wave_sem,
):
    ny, nz, nc, nx = sizes
    owners = ny * nz * nc
    _, channels, gates, pulses = raw_ref.shape
    rim = rim_in_ref.shape[2]
    most, wide = 2 * pack_ref.shape[2], pack_ref.shape[4]
    halves_sent = pack_ref.shape[0]
    some = channels // halves_sent
    dop, rng = lax.axis_index("dop"), lax.axis_index("rng")
    y, z, c = dop // (nz * nc), (dop // nc) % nz, dop % nc
    tn = ((0,), (0,))

    def owner_at(ky, kz, kc):
        return (((y + ky) % ny) * nz + (z + kz) % nz) * nc + (c + kc) % nc

    loads = [
        pltpu.make_async_copy(raw_hbm.at[:, :, :rim], raw_ref.at[:, :, :rim], load_sem.at[0]),
        pltpu.make_async_copy(high_hbm, high_ref, load_sem.at[1]),
        pltpu.make_async_copy(low_hbm, low_ref, load_sem.at[2]),
        pltpu.make_async_copy(raw_hbm.at[:, :, rim:], raw_ref.at[:, :, rim:], load_sem.at[3]),
        pltpu.make_async_copy(gates_hbm, gates_ref, load_sem.at[4]),
        pltpu.make_async_copy(pivots_hbm, pivots_ref, load_sem.at[5]),
        pltpu.make_async_copy(weights_hbm, weights_ref, load_sem.at[6]),
    ]
    for load in loads:
        load.start()

    barrier = pltpu.get_barrier_semaphore()
    along_y = [owner_at(k, 0, 0) for k in range(1, ny)]
    along_z = [owner_at(0, k, 0) for k in (2, nz - 2)]
    near = along_y + along_z + [owner_at(0, 1, 0), owner_at(0, nz - 1, 0), owner_at(0, 0, 1)]
    for other in near:
        pl.semaphore_signal(barrier, inc=1, device_id=(other, rng), device_id_type=MESH)
    for k in range(1, nx):
        pl.semaphore_signal(barrier, inc=1, device_id=(dop, (rng + k) % nx), device_id_type=MESH)
    waves = [along_z, along_y, [owner_at(0, 0, 1)]]

    def wave(number):
        for other in waves[number]:
            pl.semaphore_signal(wave_sem.at[number], inc=1, device_id=(other, rng), device_id_type=MESH)

    def wave_end(number):
        pl.semaphore_wait(wave_sem.at[number], len(waves[number]))

    loads[0].wait()
    for ch in range(channels):
        for part in range(2):
            rim_out_ref[ch, part] = raw_ref[part, ch, :rim].astype(BF16)

    pl.semaphore_wait(barrier, len(near) + nx - 1)

    @pl.when(rng > 0)
    def _():
        for ch in range(channels):
            pltpu.make_async_remote_copy(
                src_ref=rim_out_ref.at[ch], dst_ref=rim_in_ref.at[ch], send_sem=rim_send_sem.at[ch],
                recv_sem=rim_recv_sem.at[ch], device_id=(dop, rng - 1), device_id_type=MESH,
            ).start()

    @pl.when(rng == nx - 1)
    def _():
        rim_in_ref[...] = jnp.zeros_like(rim_in_ref)

    wave(0)

    own, next_ = filter_response(replica_ref, gates, rim)
    near_high, near_low = halves(own)
    far_high, far_low = halves(next_)
    for load in loads[1:4]:
        load.wait()
    for ch in range(channels):
        high, low = halves(jnp.concatenate([raw_ref[0, ch], raw_ref[1, ch]], axis=1))
        inner = dot(high, high_ref[...]) + (dot(low, high_ref[...]) + dot(high, low_ref[...]))
        high, low = halves(jnp.concatenate([inner[:, :pulses], inner[:, pulses:]], axis=0))
        part_ref[ch] = dot(high, near_high, tn) + (dot(low, near_high, tn) + dot(high, near_low, tn))

    def run(owner, total):
        starts_ref[owner] = total
        return total + counts_ref[owner]

    lax.fori_loop(0, owners, run, 0)
    loads[4].wait()
    local = gates_ref[...].T % gates
    pick_ref[...] = jnp.concatenate([local, local], axis=1)

    wave_end(0)
    wave(1)

    loads[6].wait()
    dof = pivots_ref.shape[0]
    order = 2 * dof
    lane = lax.broadcasted_iota(jnp.int32, (dof, 128), 1)
    is_real = lane % (2 * some) < some
    for half in range(halves_sent):
        index = lane // channels * channels + half * some + lane % some
        for lo in range(0, weights_ref.shape[1], 128):
            real = jnp.take_along_axis(weights_ref[:dof, lo : lo + 128].astype(F32), index, axis=1)
            imag = jnp.take_along_axis(weights_ref[dof:, lo : lo + 128].astype(F32), index, axis=1)
            mixed_ref[half, :dof, lo : lo + 128] = jnp.where(is_real, real, imag).astype(BF16)
            mixed_ref[half, dof:, lo : lo + 128] = jnp.where(is_real, -imag, real).astype(BF16)

    first_half = lax.broadcasted_iota(jnp.int32, (channels, wide), 1) < wide // 2

    def finish(ch):
        @pl.when(rng < nx - 1)
        def _():
            pltpu.make_async_copy(rim_in_ref.at[ch], rim_in_ref.at[ch], rim_recv_sem.at[ch]).wait()

        edge = jnp.concatenate([rim_in_ref[ch, 0], rim_in_ref[ch, 1]], axis=1)
        outer = dot(edge, high_ref[...]) + dot(edge, low_ref[...])
        high, low = halves(jnp.concatenate([outer[:, :pulses], outer[:, pulses:]], axis=0))
        done = dot(high, far_high, tn) + (dot(low, far_high, tn) + dot(high, far_low, tn))
        done = done + part_ref[ch]
        at = ch // some * channels + ch % some
        spec_ref[:, at, :] = done[:, :gates]
        spec_ref[:, at + some, :] = done[:, gates:]

    def packed(half, owner):
        pairs = []
        for pair in range(most // 2):
            picked = []
            for slot in (2 * pair, 2 * pair + 1):
                b = jnp.minimum(starts_ref[owner] + slot, pulses - 1)
                index = jnp.broadcast_to(pick_ref[pl.ds(b, 1), :], (channels, wide))
                picked.append(jnp.take_along_axis(spec_ref[b, half * channels : half * channels + channels], index, axis=1))
            pairs.append(jnp.where(first_half, picked[0], picked[1]).astype(BF16))
        return pairs

    def store(half, owner, pairs, ref):
        for pair in range(most // 2):
            ref[half, owner, pair] = pairs[pair]

    def send(half, owner):
        pltpu.make_async_remote_copy(
            src_ref=pack_ref.at[half, owner], dst_ref=recv_ref.at[half, dop], send_sem=send_sem.at[half],
            recv_sem=recv_sem.at[half], device_id=(owner, rng), device_id_type=MESH,
        ).start()

    away = sorted(range(nz), key=lambda k: (min(k, nz - k), k))
    for half in range(halves_sent):
        for ch in range(half * some, half * some + some):
            finish(ch)
            if ch in (1, 3):
                wave_end(ch // 2 + 1)
                if ch == 1:
                    wave(2)
        for kz in away:
            group = [owner_at(ky, kz, kc) for kc in range(nc) for ky in range(ny)]
            ready = [packed(half, owner) for owner in group]
            for number, owner in enumerate(group):
                store(half, owner, ready[number], recv_ref if kz == 0 and number == 0 else pack_ref)
            for number, owner in enumerate(group):
                if kz or number:
                    send(half, owner)

    loads[5].wait()
    slot_bin = jnp.minimum(starts_ref[dop] + rng, pulses - 1)
    full = jnp.where(rng < counts_ref[dop], 1.0, 0.0)
    pivot = jnp.take_along_axis(pivots_ref[...], jnp.full(pivots_ref.shape, slot_bin, jnp.int32), axis=1)
    pivot = jnp.concatenate([pivot, pivot], axis=1)[:, :dof]
    chooser = (lax.broadcasted_iota(jnp.int32, (dof, dof), 1) == pivot).astype(BF16)
    r_ref[...] = jnp.zeros_like(r_ref)
    rows = order // nx
    span = 32
    last = order - rows
    pieces = [(lo, lo + rows) for lo in range(0, last, rows)] + [(lo, lo + span) for lo in range(last, order, span)]
    for lo, hi in pieces:
        first = lo // 128 * 128
        if first:
            @pl.when(rng == lo // rows)
            def _():
                out_ref[:, lo % rows : lo % rows + hi - lo, :first] = jnp.zeros((nx, hi - lo, first), F32)

    sums = None
    for half in range(halves_sent):
        others = recv_ref.at[half, pl.ds(0, owners - 1)]
        pltpu.make_async_copy(others, others, recv_sem.at[half]).wait()
        data = [recv_ref[half, :, pair].reshape(owners * channels, wide) for pair in range(most // 2)]
        share = dot(mixed_ref[half], jnp.concatenate(data, axis=1))
        sums = share if sums is None else sums + share
    left = lax.broadcasted_iota(jnp.int32, (dof, wide), 1) < wide // 2
    sign = jnp.where(left, 1.0, -1.0)
    for slot in range(most):
        lo = slot // 2 * wide
        real, imag = sums[:dof, lo : lo + wide], sums[dof:, lo : lo + wide]
        if slot % 2:
            real = pltpu.roll(real, wide // 2, 1)
        else:
            imag = pltpu.roll(imag, wide // 2, 1)
        bsend_ref[slot] = jnp.where(left, real, imag).astype(BF16)
    for k in range(1, nx):
        slot = (rng + k) % nx
        pltpu.make_async_remote_copy(
            src_ref=bsend_ref.at[slot], dst_ref=brecv_ref.at[rng], send_sem=bsend_sem.at[k - 1],
            recv_sem=brecv_sem.at[k - 1], device_id=(dop, slot), device_id_type=MESH,
        ).start()
    brecv_ref[rng] = bsend_ref[rng]
    for k in range(1, nx):
        pltpu.make_async_copy(bsend_ref.at[k - 1], bsend_ref.at[k - 1], brecv_sem.at[k - 1]).wait()

    parts = [dot(chooser, brecv_ref[k]) for k in range(nx)]
    upper = jnp.concatenate(parts, axis=1)
    lower = jnp.concatenate([sign * pltpu.roll(part, wide // 2, 1) for part in parts], axis=1)
    both = jnp.concatenate([upper, lower], axis=0).astype(BF16)
    gram = dot(both, both, ((1,), (1,)))
    diagonal = lax.broadcasted_iota(jnp.int32, (order, order), 0) == lax.broadcasted_iota(jnp.int32, (order, order), 1)
    a_ref[...] = gram * (1.0 / count_rows) + jnp.where(diagonal, LOADING, 0.0)

    def source(lo, hi):
        return r_ref.at[lo:hi, lo // 128 * 128 :]

    def target(slot, lo, hi):
        return out_ref.at[slot, lo % rows : lo % rows + hi - lo, lo // 128 * 128 :]

    for r0 in range(0, order, span):
        factor_rows(a_ref, r_ref, r0, full, span)
        for number, (lo, hi) in enumerate(pieces):
            if hi == r0 + span:
                @pl.when(rng != lo // rows)
                def _():
                    pltpu.make_async_remote_copy(
                        src_ref=source(lo, hi), dst_ref=target(rng, lo, hi), send_sem=rsend_sem.at[number],
                        recv_sem=rrecv_sem.at[rng, lo % rows // span], device_id=(dop, lo // rows), device_id_type=MESH,
                    ).start()

    for half in range(halves_sent):
        others = recv_ref.at[half, pl.ds(0, owners - 1)]
        pltpu.make_async_copy(others, others, send_sem.at[half]).wait()
    for k in range(1, nx):
        pltpu.make_async_copy(bsend_ref.at[k - 1], bsend_ref.at[k - 1], bsend_sem.at[k - 1]).wait()

    @pl.when(rng > 0)
    def _():
        for ch in range(channels):
            pltpu.make_async_copy(rim_out_ref.at[ch], rim_out_ref.at[ch], rim_send_sem.at[ch]).wait()

    for r in range(nx):
        @pl.when(rng == r)
        def _():
            out_ref[r] = r_ref[rows * r : rows * r + rows]

    for number, (lo, hi) in enumerate(pieces):
        @pl.when(rng == lo // rows)
        def _():
            for slot in range(nx):
                if slot != lo // rows:
                    done = target(slot, lo, hi)
                    pltpu.make_async_copy(done, done, rrecv_sem.at[slot, lo % rows // span]).wait()

        @pl.when(rng != lo // rows)
        def _():
            pltpu.make_async_copy(source(lo, hi), source(lo, hi), rsend_sem.at[number]).wait()


def local(sizes, raw_echo, replica, beam_weights, pivots, owner_counts, train_gates):
    _, channels, gates, pulses = raw_echo.shape
    taps = replica.shape[1]
    owners = owner_counts.shape[0]
    nx = sizes[3]
    dof = pivots.shape[1]
    order = 2 * dof
    chosen = train_gates.shape[1]
    most = 2 * (pulses // owners)
    count_rows = float(chosen * nx)
    high, low = doppler_table(pulses)
    weights = beam_weights.transpose(0, 2, 1).reshape(order, -1)
    pivots, picks = pivots.T, train_gates.T
    vmem, anywhere = pl.BlockSpec(memory_space=pltpu.VMEM), pl.BlockSpec(memory_space=pl.ANY)
    dma = pltpu.SemaphoreType.DMA
    return pl.pallas_call(
        functools.partial(kernel, count_rows, sizes),
        out_shape=pltpu.VMEM((most, order // nx, order), F32),
        in_specs=[pl.BlockSpec(memory_space=pltpu.SMEM), vmem] + [anywhere] * 6,
        out_specs=vmem,
        scratch_shapes=[
            pltpu.VMEM(raw_echo.shape, F32),
            pltpu.VMEM(high.shape, BF16),
            pltpu.VMEM(low.shape, BF16),
            pltpu.VMEM(weights.shape, BF16),
            pltpu.VMEM(pivots.shape, jnp.int32),
            pltpu.VMEM(picks.shape, jnp.int32),
            pltpu.VMEM((channels, 2, taps, pulses), BF16),
            pltpu.VMEM((channels, 2, taps, pulses), BF16),
            pltpu.VMEM((channels, pulses, 2 * gates), F32),
            pltpu.VMEM((pulses, 2 * channels, gates), F32),
            pltpu.VMEM((pulses, 2 * chosen), jnp.int32),
            pltpu.SMEM((owners,), jnp.int32),
            pltpu.VMEM((2, order, weights.shape[1]), BF16),
            pltpu.VMEM((2, owners, most // 2, channels, 2 * chosen), BF16),
            pltpu.VMEM((2, owners, most // 2, channels, 2 * chosen), BF16),
            pltpu.VMEM((nx, dof, 2 * chosen), BF16),
            pltpu.VMEM((nx, dof, 2 * chosen), BF16),
            pltpu.VMEM((order, order), F32),
            pltpu.VMEM((order, order), F32),
            dma((7,)), dma((channels,)), dma((channels,)), dma((2,)), dma((2,)),
            dma((nx - 1,)), dma((nx - 1,)), dma((order // 32,)), dma((nx, order // nx // 32)),
            pltpu.SemaphoreType.REGULAR((3,)),
        ],
        compiler_params=pltpu.CompilerParams(collective_id=1, has_side_effects=True),
        name="factors",
    )(owner_counts, replica, raw_echo, jnp.asarray(high), jnp.asarray(low), weights, pivots, picks)


def solution(mesh):
    return jax.shard_map(
        functools.partial(local, (4, 8, 2, 4)),
        mesh=mesh,
        in_specs=(P(None, "dop", "rng", None), P(), P(), P(), P(), P(None, "rng")),
        out_specs=P("dop", "rng", None),
        check_vma=False,
    )
```

```python
import functools
import math

import jax
import jax.numpy as jnp
import numpy as np
from jax import lax
from jax.experimental import pallas as pl
from jax.experimental.pallas import tpu as pltpu
from jax.sharding import PartitionSpec as P

LOADING = 0.25
MESH = pl.DeviceIdType.MESH
BF16 = jnp.bfloat16
F32 = jnp.float32


def doppler_table(pulse_count):
    index = np.arange(pulse_count, dtype=np.int32)
    phase = (index[:, None] * index[None, :]) % pulse_count
    angle = phase.astype(np.float32) * np.float32(2.0 * math.pi / pulse_count)
    scale = np.float32(1.0 / math.sqrt(pulse_count))
    cos, sin = np.cos(angle) * scale, np.sin(angle) * scale
    table = np.block([[cos, -sin], [sin, cos]]).astype(np.float32)
    high = table.astype(BF16)
    low = (table - high.astype(np.float32)).astype(BF16)
    return high, low


def halves(x):
    high = x.astype(BF16)
    return high, (x - high.astype(F32)).astype(BF16)


def dot(a, b, dims=((1,), (0,))):
    return lax.dot_general(a, b, (dims, ((), ())), preferred_element_type=F32)


def factor_rows(a_ref, r_ref, r0, full, span):
    order = a_ref.shape[1]
    edge = r0 // 128 * 128
    tiles, groups = (order - edge) // 128, span // 8
    shape = (8, 128)
    sub = lax.broadcasted_iota(jnp.int32, shape, 0)
    lane = lax.broadcasted_iota(jnp.int32, shape, 1)
    p = [[a_ref[r0 + 8 * g : r0 + 8 * g + 8, edge + 128 * u : edge + 128 * u + 128] for u in range(tiles)] for g in range(groups)]

    def column(v, m):
        return jnp.take_along_axis(v, jnp.full(shape, m, jnp.int32), axis=1)

    def line(v, i):
        return jnp.broadcast_to(v[i : i + 1], shape)

    for k in range(groups):
        off = r0 - edge + 8 * k
        cols = {g: [column(p[g][0], off + m) for m in range(8)] for g in range(k + 1, groups)}
        cols[k] = ahead if k else [column(p[k][0], off + m) for m in range(8)]
        if k + 1 < groups:
            ahead = [column(p[k + 1][0], off + 8 + m) for m in range(8)]
        pivots = None
        for j in range(8):
            head = cols[k][j]
            pivot = line(head, j)
            across = {m: line(cols[k][m], j) for m in range(j + 1, 8)}
            rows = [line(p[k][u], j) for u in range(tiles)]
            inv = lax.rsqrt(pivot)
            inv2 = inv * inv
            pivots = inv if j == 0 else jnp.where(sub == j, inv, pivots)
            if j < 7:
                first = head * across[j + 1]
                cols[k][j + 1] = cols[k][j + 1] - first * inv2
                scaled = head * inv2
                for m in range(j + 2, 8):
                    cols[k][m] = cols[k][m] - scaled * across[m]
                below = jnp.where(sub > j, scaled, 0.0)
                for u in range(tiles):
                    p[k][u] = p[k][u] - below * rows[u]
            for g in range(k + 1, groups):
                scaled = cols[g][j] * inv2
                if g == k + 1:
                    for m in range(8):
                        ahead[m] = ahead[m] - scaled * line(cols[g][j], m)
                for m in range(j + 1, 8):
                    cols[g][m] = cols[g][m] - scaled * across[m]
                for u in range(tiles):
                    p[g][u] = p[g][u] - scaled * rows[u]
        for u in range(tiles):
            v = p[k][u] * pivots
            if u == 0:
                v = jnp.where(lane >= off + sub, v, 0.0)
            p[k][u] = v
            r_ref[r0 + 8 * k : r0 + 8 * k + 8, edge + 128 * u : edge + 128 * u + 128] = v * full
    rest = r0 + span
    if rest < order:
        start = rest // 128 * 128
        x = jnp.concatenate([jnp.concatenate(p[g][(start - edge) // 128 :], axis=1) for g in range(groups)], axis=0)
        high = x.astype(BF16)
        low = (x - high.astype(F32)).astype(BF16)
        update = dot(jnp.concatenate([high, high, low], axis=0), jnp.concatenate([high, low, high], axis=0), ((0,), (0,)))
        a_ref[rest:, start:] = a_ref[rest:, start:] - update[rest - start:]


def filter_response(replica_ref, gates, rim):
    taps = replica_ref.shape[1]
    lane = lax.broadcasted_iota(jnp.int32, (gates, gates), 1)
    row = lax.broadcasted_iota(jnp.int32, (gates, gates), 0)
    back = (gates - lane[:8]) % gates
    rolled = []
    for part in range(2):
        line = jnp.concatenate([replica_ref[part : part + 1], jnp.zeros((1, gates - taps), F32)], axis=1)
        line = jnp.take_along_axis(jnp.broadcast_to(line, (8, gates)), back, axis=1)
        rolled.append(pltpu.roll(jnp.broadcast_to(line[:1], (gates, gates)), 0, 1, stride=1, stride_axis=0))
    near = (row >= lane) & (row - lane < taps)
    far = (row[:rim] + gates - lane[:rim]) < taps
    re_near, im_near = [jnp.where(near, part, 0.0) for part in rolled]
    re_far, im_far = [jnp.where(far, part[:rim], 0.0) for part in rolled]
    return (
        jnp.concatenate(
            [jnp.concatenate([re_near, -im_near], axis=1), jnp.concatenate([im_near, re_near], axis=1)], axis=0
        ),
        jnp.concatenate(
            [jnp.concatenate([re_far, -im_far], axis=1), jnp.concatenate([im_far, re_far], axis=1)], axis=0
        ),
    )


def kernel(
    count_rows, sizes, counts_ref, replica_ref, raw_hbm, high_hbm, low_hbm, weights_hbm, pivots_hbm, gates_hbm, out_ref,
    raw_ref, high_ref, low_ref, weights_ref, pivots_ref, gates_ref,
    rim_out_ref, rim_in_ref, part_ref, spec_ref, pick_ref, starts_ref,
    mixed_ref, pack_ref, recv_ref, bsend_ref, brecv_ref, a_ref, r_ref,
    load_sem, rim_load_sem, rim_send_sem, rim_recv_sem, send_sem, recv_sem, bsend_sem, brecv_sem, rsend_sem, rrecv_sem, wave_sem,
):
    ny, nz, nc, nx = sizes
    owners = ny * nz * nc
    _, channels, gates, pulses = raw_ref.shape
    rim = rim_in_ref.shape[2]
    most, wide = 2 * pack_ref.shape[2], pack_ref.shape[4]
    halves_sent = pack_ref.shape[0]
    some = channels // halves_sent
    dop, rng = lax.axis_index("dop"), lax.axis_index("rng")
    y, z, c = dop // (nz * nc), (dop // nc) % nz, dop % nc
    tn = ((0,), (0,))

    def owner_at(ky, kz, kc):
        return (((y + ky) % ny) * nz + (z + kz) % nz) * nc + (c + kc) % nc

    loads = [
        pltpu.make_async_copy(high_hbm, high_ref, load_sem.at[0]),
        pltpu.make_async_copy(low_hbm, low_ref, load_sem.at[1]),
        pltpu.make_async_copy(raw_hbm.at[:, :, rim:], raw_ref.at[:, :, rim:], load_sem.at[2]),
        pltpu.make_async_copy(gates_hbm, gates_ref, load_sem.at[3]),
        pltpu.make_async_copy(pivots_hbm, pivots_ref, load_sem.at[4]),
        pltpu.make_async_copy(weights_hbm, weights_ref, load_sem.at[5]),
    ]
    rims = [
        pltpu.make_async_copy(raw_hbm.at[:, ch, :rim], raw_ref.at[:, ch, :rim], rim_load_sem.at[ch])
        for ch in range(channels)
    ]
    for load in rims + loads:
        load.start()

    barrier = pltpu.get_barrier_semaphore()
    along_y = [owner_at(k, 0, 0) for k in range(1, ny)]
    along_z = [owner_at(0, k, 0) for k in (2, nz - 2)]
    near = [owner_at(k, 0, kc) for k in range(1, ny) for kc in range(nc)] + [owner_at(0, 0, 1)]
    near += [owner_at(0, k, kc) for k in (1, 2, nz - 2, nz - 1) for kc in range(nc)]
    for other in near:
        pl.semaphore_signal(barrier, inc=1, device_id=(other, rng), device_id_type=MESH)
    for k in range(1, nx):
        pl.semaphore_signal(barrier, inc=1, device_id=(dop, (rng + k) % nx), device_id_type=MESH)
    waves = [along_z, along_y]

    def wave(number):
        for other in waves[number]:
            pl.semaphore_signal(wave_sem.at[number], inc=1, device_id=(other, rng), device_id_type=MESH)

    def wave_end(number):
        pl.semaphore_wait(wave_sem.at[number], len(waves[number]))

    pl.semaphore_wait(barrier, len(near) + nx - 1)
    wave(0)

    def send_rim(ch):
        @pl.when(rng > 0)
        def _():
            pltpu.make_async_remote_copy(
                src_ref=rim_out_ref.at[ch], dst_ref=rim_in_ref.at[ch], send_sem=rim_send_sem.at[ch],
                recv_sem=rim_recv_sem.at[ch], device_id=(dop, rng - 1), device_id_type=MESH,
            ).start()

    for ch in range(channels):
        rims[ch].wait()
        for part in range(2):
            rim_out_ref[ch, part] = raw_ref[part, ch, :rim].astype(BF16)
        if ch:
            send_rim(ch - 1)
    send_rim(channels - 1)

    @pl.when(rng == nx - 1)
    def _():
        rim_in_ref[...] = jnp.zeros_like(rim_in_ref)

    own, next_ = filter_response(replica_ref, gates, rim)
    near_high, near_low = halves(own)
    far_high, far_low = halves(next_)
    for load in loads[:3]:
        load.wait()
    for ch in range(channels):
        high, low = halves(jnp.concatenate([raw_ref[0, ch], raw_ref[1, ch]], axis=1))
        inner = dot(high, high_ref[...]) + (dot(low, high_ref[...]) + dot(high, low_ref[...]))
        high, low = halves(jnp.concatenate([inner[:, :pulses], inner[:, pulses:]], axis=0))
        part_ref[ch] = dot(high, near_high, tn) + (dot(low, near_high, tn) + dot(high, near_low, tn))

    def run(owner, total):
        starts_ref[owner] = total
        return total + counts_ref[owner]

    lax.fori_loop(0, owners, run, 0)
    loads[3].wait()
    local = gates_ref[...].T % gates
    pick_ref[...] = jnp.concatenate([local, local], axis=1)

    wave_end(0)
    wave(1)

    loads[5].wait()
    dof = pivots_ref.shape[0]
    order = 2 * dof
    lane = lax.broadcasted_iota(jnp.int32, (dof, 128), 1)
    is_real = lane % (2 * some) < some
    for half in range(halves_sent):
        index = lane // channels * channels + half * some + lane % some
        for lo in range(0, weights_ref.shape[1], 128):
            real = jnp.take_along_axis(weights_ref[:dof, lo : lo + 128].astype(F32), index, axis=1)
            imag = jnp.take_along_axis(weights_ref[dof:, lo : lo + 128].astype(F32), index, axis=1)
            mixed_ref[half, :dof, lo : lo + 128] = jnp.where(is_real, real, imag).astype(BF16)
            mixed_ref[half, dof:, lo : lo + 128] = jnp.where(is_real, -imag, real).astype(BF16)

    first_half = lax.broadcasted_iota(jnp.int32, (channels, wide), 1) < wide // 2

    def finish(ch):
        @pl.when(rng < nx - 1)
        def _():
            pltpu.make_async_copy(rim_in_ref.at[ch], rim_in_ref.at[ch], rim_recv_sem.at[ch]).wait()

        edge = jnp.concatenate([rim_in_ref[ch, 0], rim_in_ref[ch, 1]], axis=1)
        outer = dot(edge, high_ref[...]) + dot(edge, low_ref[...])
        high, low = halves(jnp.concatenate([outer[:, :pulses], outer[:, pulses:]], axis=0))
        done = dot(high, far_high, tn) + (dot(low, far_high, tn) + dot(high, far_low, tn))
        done = done + part_ref[ch]
        at = ch // some * channels + ch % some
        spec_ref[:, at, :] = done[:, :gates]
        spec_ref[:, at + some, :] = done[:, gates:]

    def packed(half, owner):
        pairs = []
        for pair in range(most // 2):
            picked = []
            for slot in (2 * pair, 2 * pair + 1):
                b = jnp.minimum(starts_ref[owner] + slot, pulses - 1)
                index = jnp.broadcast_to(pick_ref[pl.ds(b, 1), :], (channels, wide))
                picked.append(jnp.take_along_axis(spec_ref[b, half * channels : half * channels + channels], index, axis=1))
            pairs.append(jnp.where(first_half, picked[0], picked[1]).astype(BF16))
        return pairs

    def store(half, owner, pairs, ref):
        for pair in range(most // 2):
            ref[half, owner, pair] = pairs[pair]

    def send(half, owner):
        pltpu.make_async_remote_copy(
            src_ref=pack_ref.at[half, owner], dst_ref=recv_ref.at[half, dop], send_sem=send_sem.at[half],
            recv_sem=recv_sem.at[half], device_id=(owner, rng), device_id_type=MESH,
        ).start()

    away = sorted(range(nz), key=lambda k: (min(k, nz - k), k))
    for half in range(halves_sent):
        for ch in range(half * some, half * some + some):
            finish(ch)
            if ch == 2:
                wave_end(1)
        for kz in away if half else away[::-1]:
            group = [owner_at(ky, kz, kc) for kc in range(nc) for ky in range(ny)]
            ready = [packed(half, owner) for owner in group]
            for number, owner in enumerate(group):
                store(half, owner, ready[number], recv_ref if kz == 0 and number == 0 else pack_ref)
            for number, owner in enumerate(group):
                if kz or number:
                    send(half, owner)

    loads[4].wait()
    slot_bin = jnp.minimum(starts_ref[dop] + rng, pulses - 1)
    full = jnp.where(rng < counts_ref[dop], 1.0, 0.0)
    pivot = jnp.take_along_axis(pivots_ref[...], jnp.full(pivots_ref.shape, slot_bin, jnp.int32), axis=1)
    pivot = jnp.concatenate([pivot, pivot], axis=1)[:, :dof]
    chooser = (lax.broadcasted_iota(jnp.int32, (dof, dof), 1) == pivot).astype(BF16)
    r_ref[...] = jnp.zeros_like(r_ref)
    rows = order // nx
    span = 32
    last = order - rows
    pieces = [(lo, lo + rows) for lo in range(0, last, rows)] + [(lo, lo + span) for lo in range(last, order, span)]
    for lo, hi in pieces:
        first = lo // 128 * 128
        if first:
            @pl.when(rng == lo // rows)
            def _():
                out_ref[:, lo % rows : lo % rows + hi - lo, :first] = jnp.zeros((nx, hi - lo, first), F32)

    sums = None
    for half in range(halves_sent):
        others = recv_ref.at[half, pl.ds(0, owners - 1)]
        pltpu.make_async_copy(others, others, recv_sem.at[half]).wait()
        data = [recv_ref[half, :, pair].reshape(owners * channels, wide) for pair in range(most // 2)]
        share = dot(mixed_ref[half], jnp.concatenate(data, axis=1))
        sums = share if sums is None else sums + share
    left = lax.broadcasted_iota(jnp.int32, (dof, wide), 1) < wide // 2
    sign = jnp.where(left, 1.0, -1.0)
    for slot in range(most):
        lo = slot // 2 * wide
        real, imag = sums[:dof, lo : lo + wide], sums[dof:, lo : lo + wide]
        if slot % 2:
            real = pltpu.roll(real, wide // 2, 1)
        else:
            imag = pltpu.roll(imag, wide // 2, 1)
        bsend_ref[slot] = jnp.where(left, real, imag).astype(BF16)
    for k in sorted(range(1, nx), key=lambda k: -min(k, nx - k)):
        slot = (rng + k) % nx
        pltpu.make_async_remote_copy(
            src_ref=bsend_ref.at[slot], dst_ref=brecv_ref.at[rng], send_sem=bsend_sem.at[k - 1],
            recv_sem=brecv_sem.at[k - 1], device_id=(dop, slot), device_id_type=MESH,
        ).start()
    brecv_ref[rng] = bsend_ref[rng]
    for k in range(1, nx):
        pltpu.make_async_copy(bsend_ref.at[k - 1], bsend_ref.at[k - 1], brecv_sem.at[k - 1]).wait()

    parts = [dot(chooser, brecv_ref[k]) for k in range(nx)]
    upper = jnp.concatenate(parts, axis=1)
    lower = jnp.concatenate([sign * pltpu.roll(part, wide // 2, 1) for part in parts], axis=1)
    both = jnp.concatenate([upper, lower], axis=0).astype(BF16)
    gram = dot(both, both, ((1,), (1,)))
    diagonal = lax.broadcasted_iota(jnp.int32, (order, order), 0) == lax.broadcasted_iota(jnp.int32, (order, order), 1)
    a_ref[...] = gram * (1.0 / count_rows) + jnp.where(diagonal, LOADING, 0.0)

    def source(lo, hi):
        return r_ref.at[lo:hi, lo // 128 * 128 :]

    def target(slot, lo, hi):
        return out_ref.at[slot, lo % rows : lo % rows + hi - lo, lo // 128 * 128 :]

    for r0 in range(0, order, span):
        factor_rows(a_ref, r_ref, r0, full, span)
        for number, (lo, hi) in enumerate(pieces):
            if hi == r0 + span:
                @pl.when(rng != lo // rows)
                def _():
                    pltpu.make_async_remote_copy(
                        src_ref=source(lo, hi), dst_ref=target(rng, lo, hi), send_sem=rsend_sem.at[number],
                        recv_sem=rrecv_sem.at[rng, lo % rows // span], device_id=(dop, lo // rows), device_id_type=MESH,
                    ).start()

    for half in range(halves_sent):
        others = recv_ref.at[half, pl.ds(0, owners - 1)]
        pltpu.make_async_copy(others, others, send_sem.at[half]).wait()
    for k in range(1, nx):
        pltpu.make_async_copy(bsend_ref.at[k - 1], bsend_ref.at[k - 1], bsend_sem.at[k - 1]).wait()

    @pl.when(rng > 0)
    def _():
        for ch in range(channels):
            pltpu.make_async_copy(rim_out_ref.at[ch], rim_out_ref.at[ch], rim_send_sem.at[ch]).wait()

    for r in range(nx):
        @pl.when(rng == r)
        def _():
            out_ref[r] = r_ref[rows * r : rows * r + rows]

    for number, (lo, hi) in enumerate(pieces):
        @pl.when(rng == lo // rows)
        def _():
            for slot in range(nx):
                if slot != lo // rows:
                    done = target(slot, lo, hi)
                    pltpu.make_async_copy(done, done, rrecv_sem.at[slot, lo % rows // span]).wait()

        @pl.when(rng != lo // rows)
        def _():
            pltpu.make_async_copy(source(lo, hi), source(lo, hi), rsend_sem.at[number]).wait()


def local(sizes, raw_echo, replica, beam_weights, pivots, owner_counts, train_gates):
    _, channels, gates, pulses = raw_echo.shape
    taps = replica.shape[1]
    owners = owner_counts.shape[0]
    nx = sizes[3]
    dof = pivots.shape[1]
    order = 2 * dof
    chosen = train_gates.shape[1]
    most = 2 * (pulses // owners)
    count_rows = float(chosen * nx)
    high, low = doppler_table(pulses)
    weights = beam_weights.transpose(0, 2, 1).reshape(order, -1)
    pivots, picks = pivots.T, train_gates.T
    vmem, anywhere = pl.BlockSpec(memory_space=pltpu.VMEM), pl.BlockSpec(memory_space=pl.ANY)
    dma = pltpu.SemaphoreType.DMA
    return pl.pallas_call(
        functools.partial(kernel, count_rows, sizes),
        out_shape=pltpu.VMEM((most, order // nx, order), F32),
        in_specs=[pl.BlockSpec(memory_space=pltpu.SMEM), vmem] + [anywhere] * 6,
        out_specs=vmem,
        scratch_shapes=[
            pltpu.VMEM(raw_echo.shape, F32),
            pltpu.VMEM(high.shape, BF16),
            pltpu.VMEM(low.shape, BF16),
            pltpu.VMEM(weights.shape, BF16),
            pltpu.VMEM(pivots.shape, jnp.int32),
            pltpu.VMEM(picks.shape, jnp.int32),
            pltpu.VMEM((channels, 2, taps, pulses), BF16),
            pltpu.VMEM((channels, 2, taps, pulses), BF16),
            pltpu.VMEM((channels, pulses, 2 * gates), F32),
            pltpu.VMEM((pulses, 2 * channels, gates), F32),
            pltpu.VMEM((pulses, 2 * chosen), jnp.int32),
            pltpu.SMEM((owners,), jnp.int32),
            pltpu.VMEM((2, order, weights.shape[1]), BF16),
            pltpu.VMEM((2, owners, most // 2, channels, 2 * chosen), BF16),
            pltpu.VMEM((2, owners, most // 2, channels, 2 * chosen), BF16),
            pltpu.VMEM((nx, dof, 2 * chosen), BF16),
            pltpu.VMEM((nx, dof, 2 * chosen), BF16),
            pltpu.VMEM((order, order), F32),
            pltpu.VMEM((order, order), F32),
            dma((6,)), dma((channels,)), dma((channels,)), dma((channels,)), dma((2,)), dma((2,)),
            dma((nx - 1,)), dma((nx - 1,)), dma((order // 32,)), dma((nx, order // nx // 32)),
            pltpu.SemaphoreType.REGULAR((2,)),
        ],
        compiler_params=pltpu.CompilerParams(collective_id=1, has_side_effects=True),
        name="factors",
    )(owner_counts, replica, raw_echo, jnp.asarray(high), jnp.asarray(low), weights, pivots, picks)


def solution(mesh):
    return jax.shard_map(
        functools.partial(local, (4, 8, 2, 4)),
        mesh=mesh,
        in_specs=(P(None, "dop", "rng", None), P(), P(), P(), P(), P(None, "rng")),
        out_specs=P("dop", "rng", None),
        check_vma=False,
    )
```
